128 devices in a mesh: gx: 8 (over y, core), gy: 16 (over x, z).
Axes of the slice: x: 4, y: 4, z: 4, core: 2. Of those that a mesh axis runs over, the one named last changes fastest.
Arguments:
- log_perm: float32 [64, 512, 128], P('gx', 'gy'), may hold values from -4 to 4
- perturb: float32 [64, 512, 128], P('gx', 'gy'), may hold values from -6 to 6
- storage: float32 [64, 512, 128], P('gx', 'gy'), may hold values from 0.03 to 1
- base_press: float32 [2, 64, 512, 128], P(None, 'gx', 'gy'), may hold values from -6 to 6
- well_rows: float32 [16384, 512], P(('gx', 'gy')), may hold values from 0.002 to 0.02
- well_cells: int32 [16384], P(('gx', 'gy')), may hold values from 0 to 32767
- well_counts: int32 [16384], P(('gx', 'gy')), may hold values from 1 to 512, as said below
- well_owner: int32 [16384, 1], P(('gx', 'gy')), may hold values from 0 to 127; in each aligned block of 128 rows (0 to 127, 128 to 255, ...) at most 2 rows name the same one
- well_start: int32 [16384], P(('gx', 'gy')), may hold values from 0 to 1
Outputs:
- hess_action: float32 [64, 512, 128], P('gx', 'gy')
- final_change: float32 [64, 512, 128], P('gx', 'gy')
The draws below stay inside these ranges and needn't reach their ends.
Inputs may be any that keep to these rules, and one draw needn't show every extreme that they name: `well_owner`: names the device, counted as gx index times 16 plus gy index, whose tile holds the well; among the wells listed on one device no owner appears more than 2 times, and in every draw some device names some owner exactly 2 times. `well_cells`: index x * 32 * 128 + y * 128 + z of the well's cell within its owner's tile. `well_counts`: every draw has a well with all 512 samples and one with a single sample.
All inputs are finite; a program needn't handle non-finite values.
Results may differ from the reference program's by a relative error of at most 0.0001.
Values sent between devices are 32-bit elements; how exact they have to be, the bound alone decides.
A program may use at most 128 MiB of HBM per device.

```python
import math
import jax
import jax.numpy as jnp
import numpy as np

CX = 8
CY = 32
NZ = 128
TSTEPS = 2
VCYCLES = 2
SWEEPS = 2
CSWEEPS = 4
SAMPLES = 512
CAP = 2
WELLS_DEV = 128
WELLS = 16384
NX = 64
NY = 512
N_GY = 16
DEVICES = 128


def draw_well_counts(key, part):
    counts = jax.random.randint(key, (WELLS,), 1, SAMPLES + 1, dtype=jnp.int32)
    counts = counts.at[0].set(SAMPLES)
    return counts.at[1].set(1)


def touch_ends(drawn, key, low, largest):
    index_at = [jax.random.randint(jax.random.fold_in(key, axis), (), 0, length) for axis, length in enumerate(drawn.shape)]
    longest = drawn.shape.index(max(drawn.shape))
    next_to = index_at[:longest] + [(index_at[longest] + 1) % drawn.shape[longest]] + index_at[longest + 1:]
    return drawn.at[tuple(index_at)].set(low).at[tuple(next_to)].set(largest)


def block_scale(own_key, dims, split, smallest, top_value):
    def one(position, shards_of):
        draws = jax.random.uniform(jax.random.fold_in(jax.random.fold_in(own_key, 6), position), (shards_of,), jnp.float32, smallest / len(split), top_value / len(split))
        return jnp.repeat(jnp.exp(draws), dims[position] // shards_of).reshape((-1,) + (1,) * (len(dims) - position - 1))

    factor_of = one(*split[0])
    for cut in split[1:]:
        factor_of = factor_of * one(*cut)
    return factor_of


def deal_out(key, own, number, rows, amount, top, reach, slope):
    sequence = jax.random.permutation(key, amount)
    crowded, common = load_shares(amount, rows * top, reach, slope, True), load_shares(amount, rows * top, reach, slope, False)
    places = jnp.arange(amount)

    def named(sizes, rotation):
        used = int((sizes > 0).sum())
        fixed = max(1, used // 4)
        moved = fixed + (places - fixed + rotation * (used - fixed)) % max(1, amount - fixed)
        return jnp.zeros((amount,), jnp.int32).at[sequence[jnp.where(places < fixed, places, moved)]].set(jnp.asarray(sizes, jnp.int32))

    sizes = jnp.where(number % 4 == 0, named(crowded, number // 4), named(common, number - number // 4 - 1))
    mixed = jax.random.permutation(jax.random.fold_in(own, 3), amount)
    giver, taker = mixed[0:amount // 2 * 2:2], mixed[1:amount // 2 * 2:2]
    room = jnp.minimum(sizes[giver] - 1, reach - sizes[taker]) // 2
    room = jnp.where((giver == sequence[0]) | (taker == sequence[0]) | (sizes[taker] == 0), 0, jnp.maximum(room, 0))
    moved = jax.random.randint(jax.random.fold_in(own, 4), (amount // 2,), 0, 1 << 20) % (room + 1)
    sizes = sizes.at[giver].add(-moved).at[taker].add(moved)
    items = jnp.searchsorted(jnp.cumsum(sizes), jnp.arange(rows * top), side="right").astype(jnp.int32)
    table = items.reshape(top, rows).T
    table = table[jax.random.permutation(jax.random.fold_in(own, 1), rows)]
    rotation = jax.random.randint(jax.random.fold_in(own, 2), (rows, 1), 0, top)
    return jnp.take_along_axis(table, (jnp.arange(top)[None, :] + rotation) % top, axis=1)


def load_shares(number_of, total, most, lean, full):
    weights = [(1 << 20) // math.isqrt(grade ** lean) + 1 for grade in range(1, number_of + 1)]
    largest = most if full else min(most, max(-(-total // number_of), total * weights[0] // sum(weights)))
    least = 1 if total - largest >= number_of - 1 else 0
    holding, surplus = [largest] + [least] * (number_of - 1), total - largest - least * (number_of - 1)
    while surplus > 0:
        candidates = [i for i in range(1, number_of) if holding[i] < largest] or [i for i in range(1, number_of) if holding[i] < most]
        mass, remaining = sum([weights[i] for i in candidates]), surplus
        for i in candidates:
            addition = min(most - holding[i], max(1, remaining * weights[i] // mass), surplus)
            holding[i] = holding[i] + addition
            surplus = surplus - addition
    return np.array(holding)


def centred(stream_key, extent, deviation, reach, split=(), kind=jnp.bfloat16):
    factor_of = block_scale(stream_key, extent, split, -0.22, 0.18) if split else 1.0
    result = jax.random.normal(stream_key, extent, jnp.float32) * deviation * factor_of
    return jnp.minimum(jnp.maximum(result, -reach), reach).astype(kind)


def setup_inputs(seed: int = 0) -> dict:
    arg_keys = jax.random.split(jax.random.key(seed), 10)
    log_perm = centred(arg_keys[0], (NX, NY, NZ), 1.0, 4.0, ((0, 8), (1, 16)), jnp.float32)
    perturb = centred(arg_keys[1], (NX, NY, NZ), 1.0, 6.0, ((0, 8), (1, 16)), jnp.float32)
    storage = jnp.clip(jnp.exp(math.log(1.0) - 3.506558 * jax.random.uniform(arg_keys[2], (NX, NY, NZ), jnp.float32) ** block_scale(arg_keys[2], (NX, NY, NZ), ((0, 8), (1, 16)), -0.2, 0.2)), 0.03, 1.0)
    base_press = centred(arg_keys[3], (TSTEPS, NX, NY, NZ), 1.0, 6.0, ((1, 8), (2, 16)), jnp.float32)
    well_rows = jnp.clip(jnp.exp(math.log(0.02) - 2.30258502 * jax.random.uniform(arg_keys[4], (WELLS, SAMPLES), jnp.float32) ** block_scale(arg_keys[4], (WELLS, SAMPLES), ((0, 128),), -0.2, 0.2)), 0.002, 0.02)
    well_cells = touch_ends(jax.random.randint(arg_keys[5], (WELLS,), 0, CX * CY * NZ), jax.random.fold_in(arg_keys[5], 1), 0, (CX * CY * NZ) - 1).astype(jnp.int32)
    well_counts = draw_well_counts(jax.random.fold_in(arg_keys[9], 71), 0)
    well_owner_keys = jax.random.split(jax.random.fold_in(arg_keys[7], 1), WELLS // WELLS_DEV)
    well_owner_turns = jax.random.permutation(jax.random.fold_in(arg_keys[7], 3), WELLS // WELLS_DEV)
    well_owner = jax.vmap(lambda own, number: deal_out(jax.random.fold_in(arg_keys[7], 2), own, number, WELLS_DEV, DEVICES, 1, CAP, 0))(well_owner_keys, well_owner_turns).reshape((WELLS, 1))
    well_start = touch_ends(jax.random.randint(arg_keys[8], (WELLS,), 0, TSTEPS), jax.random.fold_in(arg_keys[8], 1), 0, TSTEPS - 1).astype(jnp.int32)
    return {"log_perm": log_perm, "perturb": perturb, "storage": storage, "base_press": base_press, "well_rows": well_rows, "well_cells": well_cells, "well_counts": well_counts, "well_owner": well_owner, "well_start": well_start}


OMEGA = 0.8


def lower_pad(values):
    return jnp.pad(values, ((0, 0), (0, 0), (0, 1)))


def upper_pad(values):
    return jnp.pad(values, ((0, 0), (0, 0), (1, 0)))


def zero_rim(values):
    return jnp.pad(values, ((0, 0), (1, 1), (1, 1), (0, 0)))


def coarsen(values):
    size_x, size_y, size_z = values.shape
    return values.reshape(size_x // 2, 2, size_y // 2, 2, size_z // 2, 2).mean(axis=(1, 3, 5))


def prolong(values):
    return jnp.repeat(jnp.repeat(jnp.repeat(values, 2, 0), 2, 1), 2, 2)


def coefficients(log_pad, storage_level, factor):
    center = log_pad[1:-1, 1:-1]
    along_x = factor * jnp.exp(0.5 * (log_pad[:-1, 1:-1] + log_pad[1:, 1:-1]))
    along_y = factor * jnp.exp(0.5 * (log_pad[1:-1, :-1] + log_pad[1:-1, 1:]))
    along_z = factor * jnp.exp(0.5 * (center[:, :, :-1] + center[:, :, 1:]))
    diagonal = storage_level + along_x[1:] + along_x[:-1] + along_y[:, 1:] + along_y[:, :-1]
    diagonal = diagonal + lower_pad(along_z) + upper_pad(along_z)
    return along_x, along_y, along_z, diagonal


def apply_operator(value_pad, coeffs):
    along_x, along_y, along_z, diagonal = coeffs
    center = value_pad[1:-1, 1:-1]
    beside = along_x[1:] * value_pad[2:, 1:-1] + along_x[:-1] * value_pad[:-2, 1:-1]
    beside = beside + along_y[:, 1:] * value_pad[1:-1, 2:] + along_y[:, :-1] * value_pad[1:-1, :-2]
    beside = beside + lower_pad(along_z * center[:, :, 1:]) + upper_pad(along_z * center[:, :, :-1])
    return diagonal * center - beside


def perturbed(pressure_pad, change_pad, coeffs):
    along_x, along_y, along_z, diagonal = coeffs
    pressure = pressure_pad[1:-1, 1:-1]
    change = change_pad[1:-1, 1:-1]
    summed = along_x[1:] * 0.5 * (change + change_pad[2:, 1:-1]) * (pressure - pressure_pad[2:, 1:-1])
    summed = summed + along_x[:-1] * 0.5 * (change + change_pad[:-2, 1:-1]) * (pressure - pressure_pad[:-2, 1:-1])
    summed = summed + along_y[:, 1:] * 0.5 * (change + change_pad[1:-1, 2:]) * (pressure - pressure_pad[1:-1, 2:])
    summed = summed + along_y[:, :-1] * 0.5 * (change + change_pad[1:-1, :-2]) * (pressure - pressure_pad[1:-1, :-2])
    vertical = along_z * 0.5 * (change[:, :, :-1] + change[:, :, 1:]) * (pressure[:, :, :-1] - pressure[:, :, 1:])
    return summed + lower_pad(vertical) - upper_pad(vertical)


def curvature(pressure_pad, adjoint_pad, coeffs):
    along_x, along_y, along_z, diagonal = coeffs
    pressure = pressure_pad[1:-1, 1:-1]
    adjoint = adjoint_pad[1:-1, 1:-1]
    summed = 0.5 * along_x[1:] * (pressure - pressure_pad[2:, 1:-1]) * (adjoint - adjoint_pad[2:, 1:-1])
    summed = summed + 0.5 * along_x[:-1] * (pressure - pressure_pad[:-2, 1:-1]) * (adjoint - adjoint_pad[:-2, 1:-1])
    summed = summed + 0.5 * along_y[:, 1:] * (pressure - pressure_pad[1:-1, 2:]) * (adjoint - adjoint_pad[1:-1, 2:])
    summed = summed + 0.5 * along_y[:, :-1] * (pressure - pressure_pad[1:-1, :-2]) * (adjoint - adjoint_pad[1:-1, :-2])
    vertical = 0.5 * along_z * (pressure[:, :, :-1] - pressure[:, :, 1:]) * (adjoint[:, :, :-1] - adjoint[:, :, 1:])
    return summed + lower_pad(vertical) + upper_pad(vertical)


def jacobi_sweep(iterate, right_side, coeffs, padder):
    if iterate is None:
        return OMEGA * right_side / coeffs[3]
    padded = padder(iterate[None])[0]
    return iterate + OMEGA * (right_side - apply_operator(padded, coeffs)) / coeffs[3]


def vcycle(iterate, right_side, fine_coeffs, middle_coeffs, fine_pad, middle_pad, coarse_solve):
    current = iterate
    for sweep_index in range(SWEEPS):
        current = jacobi_sweep(current, right_side, fine_coeffs, fine_pad)
    residual = right_side - apply_operator(fine_pad(current[None])[0], fine_coeffs)
    middle_side = coarsen(residual)
    middle = None
    for sweep_index in range(SWEEPS):
        middle = jacobi_sweep(middle, middle_side, middle_coeffs, middle_pad)
    middle_res = middle_side - apply_operator(middle_pad(middle[None])[0], middle_coeffs)
    middle = middle + prolong(coarse_solve(coarsen(middle_res)))
    for sweep_index in range(SWEEPS):
        middle = jacobi_sweep(middle, middle_side, middle_coeffs, middle_pad)
    current = current + prolong(middle)
    for sweep_index in range(SWEEPS):
        current = jacobi_sweep(current, right_side, fine_coeffs, fine_pad)
    return current


def multigrid_solve(right_side, fine_coeffs, middle_coeffs, fine_pad, middle_pad, coarse_solve):
    current = None
    for cycle_index in range(VCYCLES):
        current = vcycle(current, right_side, fine_coeffs, middle_coeffs, fine_pad, middle_pad, coarse_solve)
    return current


def well_weights(records, counts, starts):
    sample_pos = jnp.arange(SAMPLES, dtype=jnp.int32)
    counted = jnp.where(sample_pos[None, :] < counts[:, None], records, 0.0)
    per_step = counted.reshape(records.shape[0], TSTEPS, SAMPLES // TSTEPS).sum(axis=2)
    step_pos = jnp.arange(TSTEPS, dtype=jnp.int32)
    return jnp.where(step_pos[None, :] >= starts[:, None], per_step, 0.0)


def reference(log_perm, perturb, storage, base_press, well_rows, well_cells, well_counts, well_owner, well_start):
    padded = zero_rim(jnp.concatenate([log_perm[None], perturb[None], base_press], axis=0))
    fine_coeffs = coefficients(padded[0], storage, 1.0)
    middle_log = coarsen(log_perm)
    middle_store = coarsen(storage)
    middle_coeffs = coefficients(zero_rim(middle_log[None])[0], middle_store, 0.25)
    coarse_coeffs = coefficients(zero_rim(coarsen(middle_log)[None])[0], coarsen(middle_store), 0.0625)

    def coarse_solve(right_side):
        iterate = None
        for sweep_index in range(CSWEEPS):
            iterate = jacobi_sweep(iterate, right_side, coarse_coeffs, zero_rim)
        return iterate

    def solve_field(right_side):
        return multigrid_solve(right_side, fine_coeffs, middle_coeffs, zero_rim, zero_rim, coarse_solve)

    weights = well_weights(well_rows, well_counts, well_start)
    owner_ids = well_owner[:, 0]
    row_tile = owner_ids // N_GY
    col_tile = owner_ids % N_GY
    local_x = well_cells // (CY * NZ)
    local_y = (well_cells // NZ) % CY
    local_z = well_cells % NZ
    flat_index = ((row_tile * CX + local_x) * NY + col_tile * CY + local_y) * NZ + local_z
    source = jnp.zeros((TSTEPS, NX * NY * NZ), jnp.float32).at[:, flat_index].add(weights.T)
    source = source.reshape(TSTEPS, NX, NY, NZ)

    previous = jnp.zeros(log_perm.shape, jnp.float32)
    changes = []
    for step_index in range(TSTEPS):
        right_side = storage * previous - perturbed(padded[2 + step_index], padded[1], fine_coeffs)
        previous = solve_field(right_side)
        changes.append(previous)
    adjoint_next = jnp.zeros(log_perm.shape, jnp.float32)
    adjoints = [None] * TSTEPS
    for step_index in range(TSTEPS - 1, -1, -1):
        right_side = storage * adjoint_next + source[step_index] * changes[step_index]
        adjoint_next = solve_field(right_side)
        adjoints[step_index] = adjoint_next
    adjoint_pad = zero_rim(jnp.stack(adjoints))
    hessian = jnp.zeros(log_perm.shape, jnp.float32)
    for step_index in range(TSTEPS):
        hessian = hessian - curvature(padded[2 + step_index], adjoint_pad[step_index], fine_coeffs)
    return hessian, changes[-1]
```

```python
import jax
import jax.numpy as jnp
from jax import lax
from jax.experimental import pallas as pl
from jax.experimental.pallas import tpu as pltpu
from jax.sharding import PartitionSpec as P

TSTEPS = 2
VCYCLES = 2
SAMPLES = 512
CAP = 2
OMEGA = 0.8

F32 = jnp.float32
MESH = pl.DeviceIdType.MESH

CX0, CY0, H0, W0 = 8, 32, 5, 5
CX1, CY1, H1, W1 = 4, 16, 3, 3
CX2, CY2, H2 = 2, 8, 4
HY = 8
NX0, NY0 = CX0 + 2 * H0, CY0 + 2 * HY
NX1, NY1 = CX1 + 2 * H1, CY1 + 2 * HY
NX2, NY2 = CX2 + 2 * H2, CY2 + 2 * HY
NZ = 128

NEAR = [(dx, dy) for dx in (-1, 0, 1) for dy in (-1, 0, 1) if (dx, dy) != (0, 0)]
FACES = [(-1, 0), (1, 0), (0, -1), (0, 1)]
WIDE = [(dx, dy) for dx in (-2, -1, 0, 1, 2) for dy in (-1, 0, 1) if (dx, dy) != (0, 0)]


def span_x(dx, core, halo, width):
    if dx > 0:
        return pl.ds(halo + core - width, width), pl.ds(halo - width, width)
    if dx < 0:
        return pl.ds(halo, width), pl.ds(halo + core, width)
    return pl.ds(halo, core), pl.ds(halo, core)


def span_y(dy, core):
    if dy > 0:
        return pl.ds(core, HY), pl.ds(0, HY)
    if dy < 0:
        return pl.ds(HY, HY), pl.ds(HY + core, HY)
    return pl.ds(HY, core), pl.ds(HY, core)


def span_tile(dx):
    return pl.ds(H2, CX2), pl.ds(H2 - CX2 * dx, CX2)


def swap_pair(values, stride):
    lane = lax.broadcasted_iota(jnp.int32, values.shape, values.ndim - 1)
    axis = values.ndim - 1
    return jnp.where(
        (lane & stride) == 0,
        pltpu.roll(values, NZ - stride, axis),
        pltpu.roll(values, stride, axis),
    )


def kernel(
    gx_count,
    gy_count,
    log_ref,
    pert_ref,
    stor_ref,
    press_ref,
    src_ref,
    hess_ref,
    final_ref,
    ms0,
    ms1,
    ms2,
    pp,
    xa,
    xb,
    bb,
    a0,
    dinv0,
    dg0,
    r0,
    b1,
    e1a,
    e1b,
    a1,
    dinv1,
    dg1,
    r1,
    b2,
    e2a,
    e2b,
    a2,
    dinv2,
    pair,
    prev,
    dps,
    s_ms0,
    s_ms1,
    s_ms2,
    s_pp,
    s_bb,
    s_x,
    s_b1,
    s_b2,
):
    gx = lax.axis_index("gx")
    gy = lax.axis_index("gy")

    def exists(dx, dy):
        tx, ty = gx + dx, gy + dy
        ok = None
        for cond in (
            [tx >= 0] * (dx < 0) + [tx < gx_count] * (dx > 0)
            + [ty >= 0] * (dy < 0) + [ty < gy_count] * (dy > 0)
        ):
            ok = cond if ok is None else jnp.logical_and(ok, cond)
        return ok

    def copies(offsets, sems, views):
        made = []
        for index, (dx, dy) in enumerate(offsets):
            source, target = views(dx, dy)
            made.append(
                (
                    dx,
                    dy,
                    pltpu.make_async_remote_copy(
                        src_ref=source,
                        dst_ref=target,
                        send_sem=sems.at[0, index],
                        recv_sem=sems.at[1, index],
                        device_id=(gx + dx, gy + dy),
                        device_id_type=MESH,
                    ),
                )
            )
        return made

    def start(made):
        for dx, dy, copy in made:
            pl.when(exists(dx, dy))(copy.start)

    def finish(made):
        for dx, dy, copy in made:
            pl.when(exists(-dx, -dy))(copy.wait_recv)
        for dx, dy, copy in made:
            pl.when(exists(dx, dy))(copy.wait_send)

    def views0(ref, width):
        def at(dx, dy):
            sx, tx = span_x(dx, CX0, H0, width)
            sy, ty = span_y(dy, CY0)
            return ref.at[sx, sy], ref.at[tx, ty]

        return at

    def views0s(ref, width):
        def at(dx, dy):
            sx, tx = span_x(dx, CX0, H0, width)
            sy, ty = span_y(dy, CY0)
            return ref.at[:, sx, sy], ref.at[:, tx, ty]

        return at

    def views1(ref):
        def at(dx, dy):
            sx, tx = span_x(dx, CX1, H1, W1)
            sy, ty = span_y(dy, CY1)
            return ref.at[sx, sy], ref.at[tx, ty]

        return at

    def views1s(ref):
        def at(dx, dy):
            sx, tx = span_x(dx, CX1, H1, W1)
            sy, ty = span_y(dy, CY1)
            return ref.at[:, sx, sy], ref.at[:, tx, ty]

        return at

    def views2(ref):
        def at(dx, dy):
            sx, tx = span_tile(dx)
            sy, ty = span_y(dy, CY2)
            return ref.at[sx, sy], ref.at[tx, ty]

        return at

    def views2s(ref):
        def at(dx, dy):
            sx, tx = span_tile(dx)
            sy, ty = span_y(dy, CY2)
            return ref.at[:, sx, sy], ref.at[:, tx, ty]

        return at

    def halve(first, second, size, stride):
        pair[pl.ds(0, 2 * size), :] = first + second
        summed = pair[pl.ds(0, size, stride=2), :] + pair[pl.ds(1, size, stride=2), :]
        return 0.125 * (summed + swap_pair(summed, stride))

    def double(values, size):
        pair[pl.ds(0, size, stride=2), :] = values
        pair[pl.ds(1, size, stride=2), :] = values
        return pair[pl.ds(0, 2 * size), :]

    y0, y1, y2 = pl.ds(HY, CY0), pl.ds(HY, CY1), pl.ds(HY, CY2)

    for ref in (ms0, ms1, ms2, pp, xa, xb, bb, b1, e1a, e1b, b2, e2a, e2b, a0, a1, a2):
        ref[...] = jnp.zeros(ref.shape, F32)
    prev[...] = jnp.zeros(prev.shape, F32)
    hess_ref[...] = jnp.zeros(hess_ref.shape, F32)
    for i in range(CX0):
        ms0[0, H0 + i, y0] = log_ref[i]
        ms0[1, H0 + i, y0] = stor_ref[i]
        pp[0, H0 + i, y0] = pert_ref[i]
        pp[1, H0 + i, y0] = press_ref[0, i]
        pp[2, H0 + i, y0] = press_ref[1, i]
    for i in range(CX1):
        ms1[0, H1 + i, y1] = halve(log_ref[2 * i], log_ref[2 * i + 1], CY1, 1)
        ms1[1, H1 + i, y1] = halve(stor_ref[2 * i], stor_ref[2 * i + 1], CY1, 1)
    for i in range(CX2):
        for f in range(2):
            ms2[f, H2 + i, y2] = halve(ms1[f, H1 + 2 * i, y1], ms1[f, H1 + 2 * i + 1, y1], CY2, 2)

    barrier = pltpu.get_barrier_semaphore()
    for dx, dy in WIDE:

        @pl.when(exists(dx, dy))
        def _():
            pl.semaphore_signal(
                barrier, inc=1, device_id=(gx + dx, gy + dy), device_id_type=MESH
            )

    beside_x = 1 + jnp.minimum(gx, 2) + jnp.minimum(gx_count - 1 - gx, 2)
    beside_y = 1 + jnp.minimum(gy, 1) + jnp.minimum(gy_count - 1 - gy, 1)
    pl.semaphore_wait(barrier, beside_x * beside_y - 1)

    setup = [
        copies(NEAR, s_ms0, views0s(ms0, W0)),
        copies(WIDE, s_ms2, views2s(ms2)),
        copies(NEAR, s_ms1, views1s(ms1)),
        copies(FACES, s_pp, views0s(pp, 1)),
    ]
    for made in setup:
        start(made)
    for made in setup:
        finish(made)

    def coefficients(ms, a, dinv, dg, factor, rows, core, halo, core_y, stride):
        ny = ms.shape[2]
        row = lax.broadcasted_iota(jnp.int32, (ny, NZ), 0) - HY + gy * core_y
        inside_y = jnp.logical_and(row >= 0, row < gy_count * core_y)
        lane = lax.broadcasted_iota(jnp.int32, (ny, NZ), 1)
        for i in rows:
            m = ms[0, i]
            total = ms[1, i]
            faces = []
            for other in (
                ms[0, i - 1],
                ms[0, i + 1],
                pltpu.roll(m, 1, 0),
                pltpu.roll(m, ny - 1, 0),
                pltpu.roll(m, stride, 1),
                pltpu.roll(m, NZ - stride, 1),
            ):
                faces.append(factor * jnp.exp(0.5 * (m + other)))
            faces[4] = jnp.where(lane >= stride, faces[4], 0.0)
            faces[5] = jnp.where(lane < NZ - stride, faces[5], 0.0)
            for face in faces:
                total = total + face
            place = gx * core + (i - halo)
            inside_x = jnp.logical_and(place >= 0, place < gx_count * core)
            scale = jnp.where(jnp.logical_and(inside_y, inside_x), OMEGA / total, 0.0)
            for f in range(6):
                a[f, i] = faces[f] * scale
            if halo <= i < halo + core:
                dinv[i - halo] = scale[HY : HY + core_y]
                if dg is not None:
                    dg[i - halo] = total[HY : HY + core_y] * (1.0 / OMEGA)

    coefficients(ms0, a0, dinv0, dg0, 1.0, range(1, NX0 - 1), CX0, H0, CY0, 1)
    coefficients(ms1, a1, dinv1, dg1, 0.25, range(1, NX1 - 1), CX1, H1, CY1, 2)
    coefficients(ms2, a2, dinv2, None, 0.0625, range(1, NX2 - 1), CX2, H2, CY2, 4)

    def relaxed(src, right, a, i, stride):
        ny = src.shape[0 if src.ndim == 2 else 1]
        c = src[i]
        new = (1.0 - OMEGA) * c + right
        new = new + a[0, i] * src[i - 1] + a[1, i] * src[i + 1]
        new = new + a[2, i] * pltpu.roll(c, 1, 0) + a[3, i] * pltpu.roll(c, ny - 1, 0)
        new = new + a[4, i] * pltpu.roll(c, stride, 1) + a[5, i] * pltpu.roll(c, NZ - stride, 1)
        return c, new

    def sweep(src, dst, right, a, rows, stride):
        for i in rows:
            dst[i] = relaxed(src, right(i), a, i, stride)[1]

    def around(core, halo, extra):
        return range(halo - extra, halo + core + extra)

    b1_right = lambda i: b1[i]
    b2_right = lambda i: b2[i]

    def neighbours(ref, lead, i):
        c = ref[lead, i] if lead is not None else ref[i]
        down = ref[lead, i - 1] if lead is not None else ref[i - 1]
        up = ref[lead, i + 1] if lead is not None else ref[i + 1]
        ny = c.shape[0]
        return c, (
            down,
            up,
            pltpu.roll(c, 1, 0),
            pltpu.roll(c, ny - 1, 0),
            pltpu.roll(c, 1, 1),
            pltpu.roll(c, NZ - 1, 1),
        )

    def solve(s, carry):
        slot = lax.rem(s, 2)

        @pl.when(s < TSTEPS)
        def _():
            for i in range(CX0):
                ext = H0 + i
                change, changes = neighbours(pp, 0, ext)
                press, presses = neighbours(pp, 1 + s, ext)
                total = jnp.zeros((NY0, NZ), F32)
                for f in range(6):
                    total = total + a0[f, ext] * (0.5 * (change + changes[f])) * (press - presses[f])
                bb[slot, ext, y0] = dinv0[i] * stor_ref[i] * prev[i] - total[HY : HY + CY0]

        @pl.when(s >= TSTEPS)
        def _():
            step = 2 * TSTEPS - 1 - s
            for i in range(CX0):
                bb[slot, H0 + i, y0] = dinv0[i] * (
                    stor_ref[i] * prev[i] + src_ref[step, i] * dps[step, i]
                )

        made = copies(NEAR, s_bb, views0(bb.at[slot], W0 - 1))
        start(made)
        xa[...] = jnp.zeros(xa.shape, F32)
        finish(made)
        bb_right = lambda i: bb[slot, i]

        def cycle(c, inner):
            sweep(xa, xb, bb_right, a0, around(CX0, H0, 2), 1)
            sweep(xb, xa, bb_right, a0, around(CX0, H0, 1), 1)
            for i in range(CX0):
                old, new = relaxed(xa, bb_right(H0 + i), a0, H0 + i, 1)
                r0[i] = (new - old)[HY : HY + CY0] * dg0[i]
            for i in range(CX1):
                b1[H1 + i, y1] = dinv1[i] * halve(r0[2 * i], r0[2 * i + 1], CY1, 1)
            made = copies(NEAR, s_b1, views1(b1))
            start(made)
            finish(made)
            sweep(b1, e1b, b1_right, a1, around(CX1, H1, 2), 2)
            for i in range(CX1):
                old, new = relaxed(e1b, b1[H1 + i], a1, H1 + i, 2)
                r1[i] = (new - old)[HY : HY + CY1] * dg1[i]
            for i in range(CX2):
                b2[H2 + i, y2] = dinv2[i] * halve(r1[2 * i], r1[2 * i + 1], CY2, 2)
            made = copies(WIDE, s_b2, views2(b2))
            start(made)
            finish(made)
            sweep(b2, e2a, b2_right, a2, around(CX2, H2, 3), 4)
            sweep(e2a, e2b, b2_right, a2, around(CX2, H2, 2), 4)
            sweep(e2b, e2a, b2_right, a2, around(CX2, H2, 1), 4)
            for j in range(CX2 + 2):
                spread = double(e2a[H2 - 1 + j, pl.ds(HY // 2, CY1)], CY1)
                low = H1 - 2 + 2 * j
                e1b[low] = e1b[low] + spread
                e1b[low + 1] = e1b[low + 1] + spread
            sweep(e1b, e1a, b1_right, a1, around(CX1, H1, 1), 2)
            for i in range(CX1):
                new = relaxed(e1a, b1[H1 + i], a1, H1 + i, 2)[1]
                spread = double(new[HY : HY + CY1], CY1)
                low = H0 + 2 * i
                xa[low, y0] = xa[low, y0] + spread
                xa[low + 1, y0] = xa[low + 1, y0] + spread
            made = copies(NEAR, s_x, views0(xa, W0))
            start(made)
            finish(made)
            sweep(xa, xb, bb_right, a0, around(CX0, H0, 4), 1)
            sweep(xb, xa, bb_right, a0, around(CX0, H0, 3), 1)
            return inner

        lax.fori_loop(0, VCYCLES, cycle, 0)

        @pl.when(s < TSTEPS)
        def _():
            for i in range(CX0):
                dps[s, i] = xa[H0 + i, y0]

        for i in range(CX0):
            prev[i] = jnp.where(s == TSTEPS - 1, 0.0, xa[H0 + i, y0])

        @pl.when(s >= TSTEPS)
        def _():
            step = 2 * TSTEPS - 1 - s
            for i in range(CX0):
                ext = H0 + i
                adjoint, adjoints = neighbours(xa, None, ext)
                press, presses = neighbours(pp, 1 + step, ext)
                total = jnp.zeros((NY0, NZ), F32)
                for f in range(6):
                    total = total + a0[f, ext] * (press - presses[f]) * (adjoint - adjoints[f])
                hess_ref[i] = hess_ref[i] - 0.5 * dg0[i] * total[HY : HY + CY0]

        return carry

    lax.fori_loop(0, 2 * TSTEPS, solve, 0)
    final_ref[...] = dps[TSTEPS - 1]


def gather_source(well_rows, well_cells, well_counts, well_owner, well_start, devices):
    sample_pos = jnp.arange(SAMPLES, dtype=jnp.int32)
    span = SAMPLES // TSTEPS
    counted = jnp.where(sample_pos[None, :] < well_counts[:, None], well_rows, 0.0)
    sums = []
    for step in range(TSTEPS):
        total = jnp.sum(counted[:, step * span : (step + 1) * span], axis=1)
        sums.append(jnp.where(step >= well_start, total, 0.0))
    owner = well_owner[:, 0]
    listed = owner.shape[0]
    position = jnp.arange(listed, dtype=jnp.int32)
    same = owner[:, None] == owner[None, :]
    earlier = position[None, :] < position[:, None]
    rank = jnp.sum(jnp.logical_and(same, earlier).astype(jnp.int32), axis=1)
    slot = owner * CAP + rank
    slots = devices * CAP
    hot = jnp.arange(slots, dtype=jnp.int32)[None, :] == slot[:, None]
    fields = [well_cells.astype(F32)] + sums
    send = jnp.stack(
        [jnp.sum(jnp.where(hot, field[:, None], 0.0), axis=0) for field in fields], axis=1
    )
    got = lax.all_to_all(send, ("gx", "gy"), split_axis=0, concat_axis=0, tiled=True)
    cell = got[:, 0].astype(jnp.int32)
    column = cell // NZ
    layer = cell % NZ
    columns = jnp.arange(CX0 * CY0, dtype=jnp.int32)[:, None] == column[None, :]
    layers = (jnp.arange(NZ, dtype=jnp.int32)[None, :] == layer[:, None]).astype(F32)
    weighted = jnp.stack(
        [jnp.where(columns, got[None, :, 1 + step], 0.0) for step in range(TSTEPS)]
    )
    placed = jnp.dot(
        weighted.reshape(TSTEPS * CX0 * CY0, slots), layers, precision=lax.Precision.HIGHEST
    )
    return placed.reshape(TSTEPS, CX0, CY0, NZ)


def local(
    log_perm,
    perturb,
    storage,
    base_press,
    well_rows,
    well_cells,
    well_counts,
    well_owner,
    well_start,
):
    gx_count = lax.axis_size("gx")
    gy_count = lax.axis_size("gy")
    source = gather_source(
        well_rows, well_cells, well_counts, well_owner, well_start, gx_count * gy_count
    )
    ext0 = (NX0, NY0, NZ)
    ext1 = (NX1, NY1, NZ)
    ext2 = (NX2, NY2, NZ)
    core0 = (CX0, CY0, NZ)
    core1 = (CX1, CY1, NZ)
    core2 = (CX2, CY2, NZ)

    def vmem(*shape):
        return pltpu.VMEM(shape, F32)

    def sems(count):
        return pltpu.SemaphoreType.DMA((2, count))

    spec = pl.BlockSpec(memory_space=pltpu.VMEM)

    def body(*refs):
        kernel(gx_count, gy_count, *refs)

    return pl.pallas_call(
        body,
        out_shape=(
            jax.ShapeDtypeStruct(core0, F32),
            jax.ShapeDtypeStruct(core0, F32),
        ),
        in_specs=[spec] * 5,
        out_specs=(spec, spec),
        scratch_shapes=[
            vmem(2, *ext0),
            vmem(2, *ext1),
            vmem(2, *ext2),
            vmem(3, *ext0),
            vmem(*ext0),
            vmem(*ext0),
            vmem(2, *ext0),
            vmem(6, *ext0),
            vmem(*core0),
            vmem(*core0),
            vmem(*core0),
            vmem(*ext1),
            vmem(*ext1),
            vmem(*ext1),
            vmem(6, *ext1),
            vmem(*core1),
            vmem(*core1),
            vmem(*core1),
            vmem(*ext2),
            vmem(*ext2),
            vmem(*ext2),
            vmem(6, *ext2),
            vmem(*core2),
            vmem(CY0, NZ),
            vmem(*core0),
            vmem(TSTEPS, *core0),
            sems(len(NEAR)),
            sems(len(NEAR)),
            sems(len(WIDE)),
            sems(len(FACES)),
            sems(len(NEAR)),
            sems(len(NEAR)),
            sems(len(NEAR)),
            sems(len(WIDE)),
        ],
        compiler_params=pltpu.CompilerParams(collective_id=0, has_side_effects=True),
    )(log_perm, perturb, storage, base_press, source)


def solution(mesh):
    return jax.shard_map(
        local,
        mesh=mesh,
        in_specs=(
            P("gx", "gy", None),
            P("gx", "gy", None),
            P("gx", "gy", None),
            P(None, "gx", "gy", None),
            P(("gx", "gy"), None),
            P(("gx", "gy")),
            P(("gx", "gy")),
            P(("gx", "gy"), None),
            P(("gx", "gy")),
        ),
        out_specs=(P("gx", "gy", None), P("gx", "gy", None)),
        check_vma=False,
    )
```

```python
import jax
import jax.numpy as jnp
from jax import lax
from jax.experimental import pallas as pl
from jax.experimental.pallas import tpu as pltpu
from jax.sharding import PartitionSpec as P

TSTEPS = 2
VCYCLES = 2
SAMPLES = 512
CAP = 2
OMEGA = 0.8

F32 = jnp.float32
MESH = pl.DeviceIdType.MESH

CX0, CY0, H0, W0 = 8, 32, 5, 5
CX1, CY1, H1, W1 = 4, 16, 3, 3
CX2, CY2, H2 = 2, 8, 4
HY = 8
NX0, NY0 = CX0 + 2 * H0, CY0 + 2 * HY
NX1, NY1 = CX1 + 2 * H1, CY1 + 2 * HY
NX2, NY2 = CX2 + 2 * H2, CY2 + 2 * HY
NZ = 128

NEAR = [(dx, dy) for dx in (-1, 0, 1) for dy in (-1, 0, 1) if (dx, dy) != (0, 0)]
FACES = [(-1, 0), (1, 0), (0, -1), (0, 1)]
WIDE = [(dx, dy) for dx in (-2, -1, 0, 1, 2) for dy in (-1, 0, 1) if (dx, dy) != (0, 0)]


def span_x(dx, core, halo, width):
    if dx > 0:
        return pl.ds(halo + core - width, width), pl.ds(halo - width, width)
    if dx < 0:
        return pl.ds(halo, width), pl.ds(halo + core, width)
    return pl.ds(halo, core), pl.ds(halo, core)


def span_y(dy, core):
    if dy > 0:
        return pl.ds(core, HY), pl.ds(0, HY)
    if dy < 0:
        return pl.ds(HY, HY), pl.ds(HY + core, HY)
    return pl.ds(HY, core), pl.ds(HY, core)


def span_tile(dx):
    return pl.ds(H2, CX2), pl.ds(H2 - CX2 * dx, CX2)


def swap_pair(values, stride):
    lane = lax.broadcasted_iota(jnp.int32, values.shape, values.ndim - 1)
    axis = values.ndim - 1
    return jnp.where(
        (lane & stride) == 0,
        pltpu.roll(values, NZ - stride, axis),
        pltpu.roll(values, stride, axis),
    )


def list_wells(rows_ref, ints_ref, listed):
    wells = rows_ref.shape[0]
    lane = lax.broadcasted_iota(jnp.int32, (wells, NZ), 1).astype(F32)
    well = lax.broadcasted_iota(jnp.int32, (wells, NZ), 0).astype(F32)
    across = [
        jnp.broadcast_to(ints_ref[pl.ds(k, 1), :].astype(F32), (NZ, wells)) for k in range(4)
    ]
    cell, count, owner, begin = [jnp.transpose(values) for values in across]
    fields = [cell]
    span = SAMPLES // TSTEPS
    for step in range(TSTEPS):
        total = jnp.zeros((wells, NZ), F32)
        for first in range(step * span, (step + 1) * span, NZ):
            records = rows_ref[:, pl.ds(first, NZ)]
            total = total + jnp.where(lane + float(first) < count, records, 0.0)
        total = jnp.sum(total, axis=1, keepdims=True)
        fields.append(jnp.where(begin <= float(step), total, 0.0))
    earlier = jnp.logical_and(owner == across[2], lane < well)
    rank = jnp.sum(jnp.where(earlier, 1.0, 0.0), axis=1, keepdims=True)
    listed[...] = jnp.zeros(listed.shape, F32)
    for slot in range(CAP):
        hit = jnp.logical_and(owner == lane, rank == float(slot))
        for f, field in enumerate(fields):
            listed[pl.ds(3 * slot + f, 1), :] = jnp.sum(
                jnp.where(hit, field, 0.0), axis=0, keepdims=True
            )


def place_wells(table, src_ref):
    columns = CX0 * CY0
    column = lax.broadcasted_iota(jnp.int32, (columns, NZ), 0)
    layer = lax.broadcasted_iota(jnp.int32, (NZ, NZ), 0)
    placed = [None] * TSTEPS
    for slot in range(CAP):
        cell = table[3 * slot : 3 * slot + 1].astype(jnp.int32)
        here = column == cell // NZ
        deep = jnp.where(layer == lax.rem(cell, NZ), 1.0, 0.0)
        for step in range(TSTEPS):
            weight = table[3 * slot + 1 + step : 3 * slot + 2 + step]
            part = lax.dot_general(
                jnp.where(here, weight, 0.0),
                deep,
                (((1,), (1,)), ((), ())),
                precision=lax.Precision.HIGHEST,
                preferred_element_type=F32,
            )
            placed[step] = part if placed[step] is None else placed[step] + part
    for step in range(TSTEPS):
        src_ref[step] = placed[step].reshape(CX0, CY0, NZ)


def kernel(
    gx_count,
    gy_count,
    log_ref,
    pert_ref,
    stor_ref,
    press_ref,
    rows_ref,
    ints_ref,
    hess_ref,
    final_ref,
    ms0,
    ms1,
    ms2,
    pp,
    xa,
    xb,
    bb,
    a0,
    dinv0,
    dg0,
    r0,
    b1,
    e1a,
    e1b,
    a1,
    dinv1,
    dg1,
    r1,
    b2,
    e2a,
    e2b,
    a2,
    dinv2,
    pair,
    prev,
    dps,
    listed,
    by_row,
    sorted_ref,
    by_col,
    src_ref,
    s_ms0,
    s_ms1,
    s_ms2,
    s_pp,
    s_bb,
    s_x,
    s_b1,
    s_b2,
    s_row,
    s_col,
):
    gx = lax.axis_index("gx")
    gy = lax.axis_index("gy")

    def exists(dx, dy):
        tx, ty = gx + dx, gy + dy
        ok = None
        for cond in (
            [tx >= 0] * (dx < 0) + [tx < gx_count] * (dx > 0)
            + [ty >= 0] * (dy < 0) + [ty < gy_count] * (dy > 0)
        ):
            ok = cond if ok is None else jnp.logical_and(ok, cond)
        return ok

    def copies(offsets, sems, views):
        made = []
        for index, (dx, dy) in enumerate(offsets):
            source, target = views(dx, dy)
            made.append(
                (
                    dx,
                    dy,
                    pltpu.make_async_remote_copy(
                        src_ref=source,
                        dst_ref=target,
                        send_sem=sems.at[0, index],
                        recv_sem=sems.at[1, index],
                        device_id=(gx + dx, gy + dy),
                        device_id_type=MESH,
                    ),
                )
            )
        return made

    def start(made):
        for dx, dy, copy in made:
            pl.when(exists(dx, dy))(copy.start)

    def finish(made):
        for dx, dy, copy in made:
            pl.when(exists(-dx, -dy))(copy.wait_recv)
        for dx, dy, copy in made:
            pl.when(exists(dx, dy))(copy.wait_send)

    def spread(table, slots, sems, peers):
        return [
            pltpu.make_async_remote_copy(
                src_ref=table,
                dst_ref=slots.at[k],
                send_sem=sems.at[0, k],
                recv_sem=sems.at[1, k],
                device_id=peer,
                device_id_type=MESH,
            )
            for k, peer in enumerate(peers)
        ]

    def views0(ref, width):
        def at(dx, dy):
            sx, tx = span_x(dx, CX0, H0, width)
            sy, ty = span_y(dy, CY0)
            return ref.at[sx, sy], ref.at[tx, ty]

        return at

    def views0s(ref, width):
        def at(dx, dy):
            sx, tx = span_x(dx, CX0, H0, width)
            sy, ty = span_y(dy, CY0)
            return ref.at[:, sx, sy], ref.at[:, tx, ty]

        return at

    def views1(ref):
        def at(dx, dy):
            sx, tx = span_x(dx, CX1, H1, W1)
            sy, ty = span_y(dy, CY1)
            return ref.at[sx, sy], ref.at[tx, ty]

        return at

    def views1s(ref):
        def at(dx, dy):
            sx, tx = span_x(dx, CX1, H1, W1)
            sy, ty = span_y(dy, CY1)
            return ref.at[:, sx, sy], ref.at[:, tx, ty]

        return at

    def views2(ref):
        def at(dx, dy):
            sx, tx = span_tile(dx)
            sy, ty = span_y(dy, CY2)
            return ref.at[sx, sy], ref.at[tx, ty]

        return at

    def views2s(ref):
        def at(dx, dy):
            sx, tx = span_tile(dx)
            sy, ty = span_y(dy, CY2)
            return ref.at[:, sx, sy], ref.at[:, tx, ty]

        return at

    def halve(first, second, size, stride):
        pair[pl.ds(0, 2 * size), :] = first + second
        summed = pair[pl.ds(0, size, stride=2), :] + pair[pl.ds(1, size, stride=2), :]
        return 0.125 * (summed + swap_pair(summed, stride))

    def double(values, size):
        pair[pl.ds(0, size, stride=2), :] = values
        pair[pl.ds(1, size, stride=2), :] = values
        return pair[pl.ds(0, 2 * size), :]

    y0, y1, y2 = pl.ds(HY, CY0), pl.ds(HY, CY1), pl.ds(HY, CY2)

    for ref in (ms0, ms1, ms2, pp, xa, xb, bb, b1, e1a, e1b, b2, e2a, e2b, a0, a1, a2):
        ref[...] = jnp.zeros(ref.shape, F32)
    prev[...] = jnp.zeros(prev.shape, F32)
    hess_ref[...] = jnp.zeros(hess_ref.shape, F32)
    for i in range(CX0):
        ms0[0, H0 + i, y0] = log_ref[i]
        ms0[1, H0 + i, y0] = stor_ref[i]
        pp[0, H0 + i, y0] = pert_ref[i]
        pp[1, H0 + i, y0] = press_ref[0, i]
        pp[2, H0 + i, y0] = press_ref[1, i]
    for i in range(CX1):
        ms1[0, H1 + i, y1] = halve(log_ref[2 * i], log_ref[2 * i + 1], CY1, 1)
        ms1[1, H1 + i, y1] = halve(stor_ref[2 * i], stor_ref[2 * i + 1], CY1, 1)
    for i in range(CX2):
        for f in range(2):
            ms2[f, H2 + i, y2] = halve(ms1[f, H1 + 2 * i, y1], ms1[f, H1 + 2 * i + 1, y1], CY2, 2)

    row_peers = [(lax.rem(gx + k, gx_count), gy) for k in range(1, gx_count)]
    col_peers = [(gx, lax.rem(gy + k, gy_count)) for k in range(1, gy_count)]

    barrier = pltpu.get_barrier_semaphore()
    for peer in row_peers + col_peers:
        pl.semaphore_signal(barrier, inc=1, device_id=peer, device_id_type=MESH)
    for dx, dy in WIDE:
        if dx != 0 and dy != 0:

            @pl.when(exists(dx, dy))
            def _():
                pl.semaphore_signal(
                    barrier, inc=1, device_id=(gx + dx, gy + dy), device_id_type=MESH
                )

    beside_x = jnp.minimum(gx, 2) + jnp.minimum(gx_count - 1 - gx, 2)
    beside_y = jnp.minimum(gy, 1) + jnp.minimum(gy_count - 1 - gy, 1)
    pl.semaphore_wait(barrier, beside_x * beside_y + gx_count - 1 + gy_count - 1)

    setup = [
        copies(NEAR, s_ms0, views0s(ms0, W0)),
        copies(WIDE, s_ms2, views2s(ms2)),
        copies(NEAR, s_ms1, views1s(ms1)),
        copies(FACES, s_pp, views0s(pp, 1)),
    ]
    for made in setup:
        start(made)
    list_wells(rows_ref, ints_ref, listed)
    row_copies = spread(listed, by_row, s_row, row_peers)
    for copy in row_copies:
        copy.start()
    for made in setup:
        finish(made)

    def coefficients(ms, a, dinv, dg, factor, rows, core, halo, core_y, stride):
        ny = ms.shape[2]
        row = lax.broadcasted_iota(jnp.int32, (ny, NZ), 0) - HY + gy * core_y
        inside_y = jnp.logical_and(row >= 0, row < gy_count * core_y)
        lane = lax.broadcasted_iota(jnp.int32, (ny, NZ), 1)
        for i in rows:
            m = ms[0, i]
            total = ms[1, i]
            faces = []
            for other in (
                ms[0, i - 1],
                ms[0, i + 1],
                pltpu.roll(m, 1, 0),
                pltpu.roll(m, ny - 1, 0),
                pltpu.roll(m, stride, 1),
                pltpu.roll(m, NZ - stride, 1),
            ):
                faces.append(factor * jnp.exp(0.5 * (m + other)))
            faces[4] = jnp.where(lane >= stride, faces[4], 0.0)
            faces[5] = jnp.where(lane < NZ - stride, faces[5], 0.0)
            for face in faces:
                total = total + face
            place = gx * core + (i - halo)
            inside_x = jnp.logical_and(place >= 0, place < gx_count * core)
            scale = jnp.where(jnp.logical_and(inside_y, inside_x), OMEGA / total, 0.0)
            for f in range(6):
                a[f, i] = faces[f] * scale
            if halo <= i < halo + core:
                dinv[i - halo] = scale[HY : HY + core_y]
                if dg is not None:
                    dg[i - halo] = total[HY : HY + core_y] * (1.0 / OMEGA)

    coefficients(ms0, a0, dinv0, dg0, 1.0, range(1, NX0 - 1), CX0, H0, CY0, 1)
    coefficients(ms1, a1, dinv1, dg1, 0.25, range(1, NX1 - 1), CX1, H1, CY1, 2)
    coefficients(ms2, a2, dinv2, None, 0.0625, range(1, NX2 - 1), CX2, H2, CY2, 4)

    def relaxed(src, right, a, i, stride):
        ny = src.shape[0 if src.ndim == 2 else 1]
        c = src[i]
        new = (1.0 - OMEGA) * c + right
        new = new + a[0, i] * src[i - 1] + a[1, i] * src[i + 1]
        new = new + a[2, i] * pltpu.roll(c, 1, 0) + a[3, i] * pltpu.roll(c, ny - 1, 0)
        new = new + a[4, i] * pltpu.roll(c, stride, 1) + a[5, i] * pltpu.roll(c, NZ - stride, 1)
        return c, new

    def sweep(src, dst, right, a, rows, stride):
        for i in rows:
            dst[i] = relaxed(src, right(i), a, i, stride)[1]

    def around(core, halo, extra):
        return range(halo - extra, halo + core + extra)

    b1_right = lambda i: b1[i]
    b2_right = lambda i: b2[i]

    def neighbours(ref, lead, i):
        c = ref[lead, i] if lead is not None else ref[i]
        down = ref[lead, i - 1] if lead is not None else ref[i - 1]
        up = ref[lead, i + 1] if lead is not None else ref[i + 1]
        ny = c.shape[0]
        return c, (
            down,
            up,
            pltpu.roll(c, 1, 0),
            pltpu.roll(c, ny - 1, 0),
            pltpu.roll(c, 1, 1),
            pltpu.roll(c, NZ - 1, 1),
        )

    col_copies = spread(sorted_ref, by_col, s_col, col_peers)

    def solve(s, carry):
        slot = lax.rem(s, 2)

        @pl.when(s < TSTEPS)
        def _():
            for i in range(CX0):
                ext = H0 + i
                change, changes = neighbours(pp, 0, ext)
                press, presses = neighbours(pp, 1 + s, ext)
                total = jnp.zeros((NY0, NZ), F32)
                for f in range(6):
                    total = total + a0[f, ext] * (0.5 * (change + changes[f])) * (press - presses[f])
                bb[slot, ext, y0] = dinv0[i] * stor_ref[i] * prev[i] - total[HY : HY + CY0]

        @pl.when(s >= TSTEPS)
        def _():
            step = 2 * TSTEPS - 1 - s
            for i in range(CX0):
                bb[slot, H0 + i, y0] = dinv0[i] * (
                    stor_ref[i] * prev[i] + src_ref[step, i] * dps[step, i]
                )

        made = copies(NEAR, s_bb, views0(bb.at[slot], W0 - 1))
        start(made)
        xa[...] = jnp.zeros(xa.shape, F32)
        finish(made)
        bb_right = lambda i: bb[slot, i]

        def cycle(c, inner):
            sweep(xa, xb, bb_right, a0, around(CX0, H0, 2), 1)
            sweep(xb, xa, bb_right, a0, around(CX0, H0, 1), 1)
            for i in range(CX0):
                old, new = relaxed(xa, bb_right(H0 + i), a0, H0 + i, 1)
                r0[i] = (new - old)[HY : HY + CY0] * dg0[i]
            for i in range(CX1):
                b1[H1 + i, y1] = dinv1[i] * halve(r0[2 * i], r0[2 * i + 1], CY1, 1)
            made = copies(NEAR, s_b1, views1(b1))
            start(made)
            finish(made)
            sweep(b1, e1b, b1_right, a1, around(CX1, H1, 2), 2)
            for i in range(CX1):
                old, new = relaxed(e1b, b1[H1 + i], a1, H1 + i, 2)
                r1[i] = (new - old)[HY : HY + CY1] * dg1[i]
            for i in range(CX2):
                b2[H2 + i, y2] = dinv2[i] * halve(r1[2 * i], r1[2 * i + 1], CY2, 2)
            made = copies(WIDE, s_b2, views2(b2))
            start(made)
            finish(made)
            sweep(b2, e2a, b2_right, a2, around(CX2, H2, 3), 4)
            sweep(e2a, e2b, b2_right, a2, around(CX2, H2, 2), 4)
            sweep(e2b, e2a, b2_right, a2, around(CX2, H2, 1), 4)
            for j in range(CX2 + 2):
                spread = double(e2a[H2 - 1 + j, pl.ds(HY // 2, CY1)], CY1)
                low = H1 - 2 + 2 * j
                e1b[low] = e1b[low] + spread
                e1b[low + 1] = e1b[low + 1] + spread
            sweep(e1b, e1a, b1_right, a1, around(CX1, H1, 1), 2)
            for i in range(CX1):
                new = relaxed(e1a, b1[H1 + i], a1, H1 + i, 2)[1]
                spread = double(new[HY : HY + CY1], CY1)
                low = H0 + 2 * i
                xa[low, y0] = xa[low, y0] + spread
                xa[low + 1, y0] = xa[low + 1, y0] + spread
            made = copies(NEAR, s_x, views0(xa, W0))
            start(made)
            finish(made)
            sweep(xa, xb, bb_right, a0, around(CX0, H0, 4), 1)
            sweep(xb, xa, bb_right, a0, around(CX0, H0, 3), 1)
            return inner

        lax.fori_loop(0, VCYCLES, cycle, 0)

        @pl.when(s < TSTEPS)
        def _():
            for i in range(CX0):
                dps[s, i] = xa[H0 + i, y0]

        @pl.when(s == 0)
        def _():
            for copy in row_copies:
                copy.wait()
            lane = lax.broadcasted_iota(jnp.int32, (8, NZ), 1)
            total = jnp.zeros((8, NZ), F32)
            for k in range(gx_count):
                table = listed[...] if k == 0 else by_row[k - 1]
                owned = jnp.where(lane // gy_count == gx, table, 0.0)
                sender = lax.rem(gx + gx_count - k, gx_count)
                shift = lax.rem((sender - gx + gx_count) * gy_count, NZ)
                total = total + pltpu.roll(owned, shift, 1)
            sorted_ref[...] = total
            for copy in col_copies:
                copy.start()

        @pl.when(s == TSTEPS - 1)
        def _():
            for copy in col_copies:
                copy.wait()
            lane = lax.broadcasted_iota(jnp.int32, (8, NZ), 1)
            mine = lax.rem(lane, gy_count) == gy
            total = jnp.zeros((8, NZ), F32)
            for k in range(gy_count):
                table = sorted_ref[...] if k == 0 else by_col[k - 1]
                sender = lax.rem(gy + gy_count - k, gy_count)
                shift = lax.rem(sender - gy + NZ, NZ)
                total = total + pltpu.roll(jnp.where(mine, table, 0.0), shift, 1)
            place_wells(total, src_ref)

        for i in range(CX0):
            prev[i] = jnp.where(s == TSTEPS - 1, 0.0, xa[H0 + i, y0])

        @pl.when(s >= TSTEPS)
        def _():
            step = 2 * TSTEPS - 1 - s
            for i in range(CX0):
                ext = H0 + i
                adjoint, adjoints = neighbours(xa, None, ext)
                press, presses = neighbours(pp, 1 + step, ext)
                total = jnp.zeros((NY0, NZ), F32)
                for f in range(6):
                    total = total + a0[f, ext] * (press - presses[f]) * (adjoint - adjoints[f])
                hess_ref[i] = hess_ref[i] - 0.5 * dg0[i] * total[HY : HY + CY0]

        return carry

    lax.fori_loop(0, 2 * TSTEPS, solve, 0)
    final_ref[...] = dps[TSTEPS - 1]


def local(
    log_perm,
    perturb,
    storage,
    base_press,
    well_rows,
    well_cells,
    well_counts,
    well_owner,
    well_start,
):
    gx_count = lax.axis_size("gx")
    gy_count = lax.axis_size("gy")
    ints = jnp.stack([well_cells, well_counts, well_owner[:, 0], well_start])
    ext0 = (NX0, NY0, NZ)
    ext1 = (NX1, NY1, NZ)
    ext2 = (NX2, NY2, NZ)
    core0 = (CX0, CY0, NZ)
    core1 = (CX1, CY1, NZ)
    core2 = (CX2, CY2, NZ)

    def vmem(*shape):
        return pltpu.VMEM(shape, F32)

    def sems(count):
        return pltpu.SemaphoreType.DMA((2, count))

    spec = pl.BlockSpec(memory_space=pltpu.VMEM)

    def body(*refs):
        kernel(gx_count, gy_count, *refs)

    return pl.pallas_call(
        body,
        out_shape=(
            jax.ShapeDtypeStruct(core0, F32),
            jax.ShapeDtypeStruct(core0, F32),
        ),
        in_specs=[spec] * 6,
        out_specs=(spec, spec),
        scratch_shapes=[
            vmem(2, *ext0),
            vmem(2, *ext1),
            vmem(2, *ext2),
            vmem(3, *ext0),
            vmem(*ext0),
            vmem(*ext0),
            vmem(2, *ext0),
            vmem(6, *ext0),
            vmem(*core0),
            vmem(*core0),
            vmem(*core0),
            vmem(*ext1),
            vmem(*ext1),
            vmem(*ext1),
            vmem(6, *ext1),
            vmem(*core1),
            vmem(*core1),
            vmem(*core1),
            vmem(*ext2),
            vmem(*ext2),
            vmem(*ext2),
            vmem(6, *ext2),
            vmem(*core2),
            vmem(CY0, NZ),
            vmem(*core0),
            vmem(TSTEPS, *core0),
            vmem(8, NZ),
            vmem(gx_count - 1, 8, NZ),
            vmem(8, NZ),
            vmem(gy_count - 1, 8, NZ),
            vmem(TSTEPS, *core0),
            sems(len(NEAR)),
            sems(len(NEAR)),
            sems(len(WIDE)),
            sems(len(FACES)),
            sems(len(NEAR)),
            sems(len(NEAR)),
            sems(len(NEAR)),
            sems(len(WIDE)),
            sems(gx_count - 1),
            sems(gy_count - 1),
        ],
        compiler_params=pltpu.CompilerParams(collective_id=0, has_side_effects=True),
    )(log_perm, perturb, storage, base_press, well_rows, ints)


def solution(mesh):
    return jax.shard_map(
        local,
        mesh=mesh,
        in_specs=(
            P("gx", "gy", None),
            P("gx", "gy", None),
            P("gx", "gy", None),
            P(None, "gx", "gy", None),
            P(("gx", "gy"), None),
            P(("gx", "gy")),
            P(("gx", "gy")),
            P(("gx", "gy"), None),
            P(("gx", "gy")),
        ),
        out_specs=(P("gx", "gy", None), P("gx", "gy", None)),
        check_vma=False,
    )
```

```python
import jax
import jax.numpy as jnp
from jax import lax
from jax.experimental import pallas as pl
from jax.experimental.pallas import tpu as pltpu
from jax.sharding import PartitionSpec as P

TSTEPS = 2
VCYCLES = 2
SAMPLES = 512
CAP = 2
OMEGA = 0.8

F32 = jnp.float32
MESH = pl.DeviceIdType.MESH

CX0, CY0, H0, W0 = 8, 32, 5, 5
CX1, CY1, H1, W1 = 4, 16, 3, 3
CX2, CY2, H2 = 2, 8, 4
HY = 8
NX0, NY0 = CX0 + 2 * H0, CY0 + 2 * HY
NX1, NY1 = CX1 + 2 * H1, CY1 + 2 * HY
NX2, NY2 = CX2 + 2 * H2, CY2 + 2 * HY
NZ = 128


def ordered(offsets):
    return sorted(offsets, key=lambda o: (o[1] == 0, -abs(o[0]), o))


NEAR = ordered([(dx, dy) for dx in (-1, 0, 1) for dy in (-1, 0, 1) if (dx, dy) != (0, 0)])
WIDE = ordered([(dx, dy) for dx in (-2, -1, 0, 1, 2) for dy in (-1, 0, 1) if (dx, dy) != (0, 0)])


def span_x(dx, core, halo, width):
    if dx > 0:
        return pl.ds(halo + core - width, width), pl.ds(halo - width, width)
    if dx < 0:
        return pl.ds(halo, width), pl.ds(halo + core, width)
    return pl.ds(halo, core), pl.ds(halo, core)


def span_y(dy, core, width):
    if dy > 0:
        return pl.ds(HY + core - width, width), pl.ds(HY - width, width)
    if dy < 0:
        return pl.ds(HY, width), pl.ds(HY + core, width)
    return pl.ds(HY, core), pl.ds(HY, core)


def strips(ref, core_x, halo, width, core_y):
    def at(dx, dy):
        if dx != 0 and dy != 0:
            deep, rows = width - 1, 4 * -(-(width - 1) // 4)
        else:
            deep, rows = width, 4 * -(-width // 4)
        sx, tx = span_x(dx, core_x, halo, deep)
        sy, ty = span_y(dy, core_y, rows)
        if len(ref.shape) == 4:
            return ref.at[:, sx, sy], ref.at[:, tx, ty]
        return ref.at[sx, sy], ref.at[tx, ty]

    return at


def tiles(ref):
    def at(dx, dy):
        sx, tx = pl.ds(H2, CX2), pl.ds(H2 - CX2 * dx, CX2)
        sy, ty = span_y(dy, CY2, 4)
        if len(ref.shape) == 4:
            return ref.at[:, sx, sy], ref.at[:, tx, ty]
        return ref.at[sx, sy], ref.at[tx, ty]

    return at


def swap_pair(values, stride):
    lane = lax.broadcasted_iota(jnp.int32, values.shape, values.ndim - 1)
    axis = values.ndim - 1
    return jnp.where(
        (lane & stride) == 0,
        pltpu.roll(values, NZ - stride, axis),
        pltpu.roll(values, stride, axis),
    )


def list_wells(rows_ref, ints_ref, listed):
    wells = rows_ref.shape[0]
    lane = lax.broadcasted_iota(jnp.int32, (wells, NZ), 1).astype(F32)
    well = lax.broadcasted_iota(jnp.int32, (wells, NZ), 0).astype(F32)
    across = [
        jnp.broadcast_to(ints_ref[pl.ds(k, 1), :].astype(F32), (NZ, wells)) for k in range(4)
    ]
    cell, count, owner, begin = [jnp.transpose(values) for values in across]
    fields = [cell]
    span = SAMPLES // TSTEPS
    for step in range(TSTEPS):
        total = jnp.zeros((wells, NZ), F32)
        for first in range(step * span, (step + 1) * span, NZ):
            records = rows_ref[:, pl.ds(first, NZ)]
            total = total + jnp.where(lane + float(first) < count, records, 0.0)
        total = jnp.sum(total, axis=1, keepdims=True)
        fields.append(jnp.where(begin <= float(step), total, 0.0))
    earlier = jnp.logical_and(owner == across[2], lane < well)
    rank = jnp.sum(jnp.where(earlier, 1.0, 0.0), axis=1, keepdims=True)
    listed[...] = jnp.zeros(listed.shape, F32)
    for slot in range(CAP):
        hit = jnp.logical_and(owner == lane, rank == float(slot))
        for f, field in enumerate(fields):
            listed[pl.ds(3 * slot + f, 1), :] = jnp.sum(
                jnp.where(hit, field, 0.0), axis=0, keepdims=True
            )


def place_wells(table, src_ref):
    columns = CX0 * CY0
    column = lax.broadcasted_iota(jnp.int32, (columns, NZ), 0)
    layer = lax.broadcasted_iota(jnp.int32, (NZ, NZ), 0)
    placed = [None] * TSTEPS
    for slot in range(CAP):
        cell = table[3 * slot : 3 * slot + 1].astype(jnp.int32)
        here = column == cell // NZ
        deep = jnp.where(layer == lax.rem(cell, NZ), 1.0, 0.0)
        for step in range(TSTEPS):
            weight = table[3 * slot + 1 + step : 3 * slot + 2 + step]
            part = lax.dot_general(
                jnp.where(here, weight, 0.0),
                deep,
                (((1,), (1,)), ((), ())),
                precision=lax.Precision.HIGHEST,
                preferred_element_type=F32,
            )
            placed[step] = part if placed[step] is None else placed[step] + part
    for step in range(TSTEPS):
        src_ref[step, pl.ds(H0, CX0), pl.ds(HY, CY0)] = placed[step].reshape(CX0, CY0, NZ)


def kernel(
    gx_count,
    gy_count,
    log_ref,
    pert_ref,
    stor_ref,
    press_ref,
    rows_ref,
    ints_ref,
    hess_ref,
    final_ref,
    ms0,
    ms1,
    ms2,
    pp,
    xa,
    xb,
    bb,
    a0,
    dinv0,
    dg0,
    r0,
    b1,
    e1a,
    e1b,
    a1,
    dinv1,
    dg1,
    r1,
    b2,
    e2a,
    e2b,
    a2,
    dinv2,
    pair,
    bl,
    dps,
    listed,
    by_row,
    sorted_ref,
    by_col,
    src_ref,
    s_ms0,
    s_ms1,
    s_ms2,
    s_pp,
    s_bb,
    s_x,
    s_b1,
    s_b2,
    s_row,
    s_col,
    s_src,
):
    gx = lax.axis_index("gx")
    gy = lax.axis_index("gy")

    def exists(dx, dy):
        tx, ty = gx + dx, gy + dy
        ok = None
        for cond in (
            [tx >= 0] * (dx < 0) + [tx < gx_count] * (dx > 0)
            + [ty >= 0] * (dy < 0) + [ty < gy_count] * (dy > 0)
        ):
            ok = cond if ok is None else jnp.logical_and(ok, cond)
        return ok

    def copies(offsets, sems, views):
        made = []
        for index, (dx, dy) in enumerate(offsets):
            source, target = views(dx, dy)
            made.append(
                (
                    dx,
                    dy,
                    pltpu.make_async_remote_copy(
                        src_ref=source,
                        dst_ref=target,
                        send_sem=sems.at[0, index],
                        recv_sem=sems.at[1, index],
                        device_id=(gx + dx, gy + dy),
                        device_id_type=MESH,
                    ),
                )
            )
        return made

    def start(made):
        for dx, dy, copy in made:
            pl.when(exists(dx, dy))(copy.start)

    def finish(made):
        for dx, dy, copy in made:
            pl.when(exists(-dx, -dy))(copy.wait_recv)
        for dx, dy, copy in made:
            pl.when(exists(dx, dy))(copy.wait_send)

    def spread(table, slots, sems, peers):
        return [
            pltpu.make_async_remote_copy(
                src_ref=table,
                dst_ref=slots.at[k],
                send_sem=sems.at[0, k],
                recv_sem=sems.at[1, k],
                device_id=peer,
                device_id_type=MESH,
            )
            for k, peer in enumerate(peers)
        ]

    def fine(ref, width):
        return strips(ref, CX0, H0, width, CY0)

    def middle(ref):
        return strips(ref, CX1, H1, W1, CY1)

    def halve(first, second, size, stride):
        pair[pl.ds(0, 2 * size), :] = first + second
        summed = pair[pl.ds(0, size, stride=2), :] + pair[pl.ds(1, size, stride=2), :]
        return 0.125 * (summed + swap_pair(summed, stride))

    def double(values, size):
        pair[pl.ds(0, size, stride=2), :] = values
        pair[pl.ds(1, size, stride=2), :] = values
        return pair[pl.ds(0, 2 * size), :]

    y0, y1, y2 = pl.ds(HY, CY0), pl.ds(HY, CY1), pl.ds(HY, CY2)

    for ref in (ms0, ms1, ms2, pp, xa, xb, bb, b1, e1a, e1b, b2, e2a, e2b, a0, a1, a2, bl, dps, src_ref, dinv0):
        ref[...] = jnp.zeros(ref.shape, F32)
    hess_ref[...] = jnp.zeros(hess_ref.shape, F32)
    for i in range(CX0):
        ms0[0, H0 + i, y0] = log_ref[i]
        ms0[1, H0 + i, y0] = stor_ref[i]
        pp[0, H0 + i, y0] = pert_ref[i]
        pp[1, H0 + i, y0] = press_ref[0, i]
        pp[2, H0 + i, y0] = press_ref[1, i]
    for i in range(CX1):
        ms1[0, H1 + i, y1] = halve(log_ref[2 * i], log_ref[2 * i + 1], CY1, 1)
        ms1[1, H1 + i, y1] = halve(stor_ref[2 * i], stor_ref[2 * i + 1], CY1, 1)
    for i in range(CX2):
        for f in range(2):
            ms2[f, H2 + i, y2] = halve(ms1[f, H1 + 2 * i, y1], ms1[f, H1 + 2 * i + 1, y1], CY2, 2)

    row_peers = [(lax.rem(gx + k, gx_count), gy) for k in range(1, gx_count)]
    col_peers = [(gx, lax.rem(gy + k, gy_count)) for k in range(1, gy_count)]

    barrier = pltpu.get_barrier_semaphore()
    for peer in row_peers + col_peers:
        pl.semaphore_signal(barrier, inc=1, device_id=peer, device_id_type=MESH)
    for dx, dy in WIDE:
        if dx != 0 and dy != 0:

            @pl.when(exists(dx, dy))
            def _():
                pl.semaphore_signal(
                    barrier, inc=1, device_id=(gx + dx, gy + dy), device_id_type=MESH
                )

    beside_x = jnp.minimum(gx, 2) + jnp.minimum(gx_count - 1 - gx, 2)
    beside_y = jnp.minimum(gy, 1) + jnp.minimum(gy_count - 1 - gy, 1)
    pl.semaphore_wait(barrier, beside_x * beside_y + gx_count - 1 + gy_count - 1)

    setup = [
        copies(NEAR, s_ms0, fine(ms0, W0)),
        copies(WIDE, s_ms2, tiles(ms2)),
        copies(NEAR, s_ms1, middle(ms1)),
        copies(NEAR, s_pp, fine(pp, 3)),
    ]
    for made in setup:
        start(made)
    list_wells(rows_ref, ints_ref, listed)
    row_copies = spread(listed, by_row, s_row, row_peers)
    for copy in row_copies:
        copy.start()
    for made in setup:
        finish(made)

    def coefficients(ms, a, dinv, dg, factor, rows, core, halo, core_y, stride):
        ny = ms.shape[2]
        row = lax.broadcasted_iota(jnp.int32, (ny, NZ), 0) - HY + gy * core_y
        inside_y = jnp.logical_and(row >= 0, row < gy_count * core_y)
        lane = lax.broadcasted_iota(jnp.int32, (ny, NZ), 1)
        for i in rows:
            m = ms[0, i]
            total = ms[1, i]
            faces = []
            for other in (
                ms[0, i - 1],
                ms[0, i + 1],
                pltpu.roll(m, 1, 0),
                pltpu.roll(m, ny - 1, 0),
                pltpu.roll(m, stride, 1),
                pltpu.roll(m, NZ - stride, 1),
            ):
                faces.append(factor * jnp.exp(0.5 * (m + other)))
            faces[4] = jnp.where(lane >= stride, faces[4], 0.0)
            faces[5] = jnp.where(lane < NZ - stride, faces[5], 0.0)
            for face in faces:
                total = total + face
            place = gx * core + (i - halo)
            inside_x = jnp.logical_and(place >= 0, place < gx_count * core)
            scale = jnp.where(jnp.logical_and(inside_y, inside_x), OMEGA / total, 0.0)
            for f in range(6):
                a[f, i] = faces[f] * scale
            if core == CX0:
                dinv[i] = scale
            elif halo <= i < halo + core:
                dinv[i - halo] = scale[HY : HY + core_y]
            if halo <= i < halo + core:
                if dg is not None:
                    dg[i - halo] = total[HY : HY + core_y] * (1.0 / OMEGA)

    coefficients(ms0, a0, dinv0, dg0, 1.0, range(1, NX0 - 1), CX0, H0, CY0, 1)
    coefficients(ms1, a1, dinv1, dg1, 0.25, range(1, NX1 - 1), CX1, H1, CY1, 2)
    coefficients(ms2, a2, dinv2, None, 0.0625, range(1, NX2 - 1), CX2, H2, CY2, 4)

    def relaxed(src, right, a, i, stride):
        ny = src.shape[0 if src.ndim == 2 else 1]
        c = src[i]
        new = (1.0 - OMEGA) * c + right
        new = new + a[0, i] * src[i - 1] + a[1, i] * src[i + 1]
        new = new + a[2, i] * pltpu.roll(c, 1, 0) + a[3, i] * pltpu.roll(c, ny - 1, 0)
        new = new + a[4, i] * pltpu.roll(c, stride, 1) + a[5, i] * pltpu.roll(c, NZ - stride, 1)
        return c, new

    def sweep(src, dst, right, a, rows, stride):
        for i in rows:
            dst[i] = relaxed(src, right(i), a, i, stride)[1]

    def around(core, halo, extra):
        return range(halo - extra, halo + core + extra)

    bb_right = lambda i: bl[i]
    b1_right = lambda i: b1[i]
    b2_right = lambda i: b2[i]

    def neighbours(ref, lead, i):
        c = ref[lead, i] if lead is not None else ref[i]
        down = ref[lead, i - 1] if lead is not None else ref[i - 1]
        up = ref[lead, i + 1] if lead is not None else ref[i + 1]
        ny = c.shape[0]
        return c, (
            down,
            up,
            pltpu.roll(c, 1, 0),
            pltpu.roll(c, ny - 1, 0),
            pltpu.roll(c, 1, 1),
            pltpu.roll(c, NZ - 1, 1),
        )

    col_copies = spread(sorted_ref, by_col, s_col, col_peers)
    src_copies = copies(NEAR, s_src, fine(src_ref, 2))

    def solve(s, carry):
        @pl.when(s < TSTEPS)
        def _():
            for i in around(CX0, H0, 2):
                change, changes = neighbours(pp, 0, i)
                press, presses = neighbours(pp, 1 + s, i)
                total = dinv0[i] * (ms0[1, i] * xa[i])
                for f in range(6):
                    total = total - a0[f, i] * (0.5 * (change + changes[f])) * (press - presses[f])
                bl[i] = total

        @pl.when(s >= TSTEPS)
        def _():
            step = 2 * TSTEPS - 1 - s
            for i in around(CX0, H0, 2):
                bl[i] = dinv0[i] * (ms0[1, i] * xa[i] + src_ref[step, i] * dps[step, i])

        for i in around(CX0, H0, 0):
            bb[i, y0] = bl[i, y0]
        xa[...] = jnp.zeros(xa.shape, F32)
        bb_copies = copies(NEAR, s_bb, fine(bb, W0 - 1))

        def cycle(c, inner):
            sweep(xa, xb, bb_right, a0, around(CX0, H0, 2), 1)
            sweep(xb, xa, bb_right, a0, around(CX0, H0, 1), 1)
            for i in range(CX0):
                old, new = relaxed(xa, bb_right(H0 + i), a0, H0 + i, 1)
                r0[i] = (new - old)[HY : HY + CY0] * dg0[i]
            for i in range(CX1):
                b1[H1 + i, y1] = dinv1[i] * halve(r0[2 * i], r0[2 * i + 1], CY1, 1)
            made = copies(NEAR, s_b1, middle(b1))
            start(made)

            @pl.when(c == 0)
            def _():
                start(bb_copies)

            finish(made)
            sweep(b1, e1b, b1_right, a1, around(CX1, H1, 2), 2)
            for i in range(CX1):
                old, new = relaxed(e1b, b1[H1 + i], a1, H1 + i, 2)
                r1[i] = (new - old)[HY : HY + CY1] * dg1[i]
            for i in range(CX2):
                b2[H2 + i, y2] = dinv2[i] * halve(r1[2 * i], r1[2 * i + 1], CY2, 2)
            made = copies(WIDE, s_b2, tiles(b2))
            start(made)
            finish(made)
            sweep(b2, e2a, b2_right, a2, around(CX2, H2, 3), 4)
            sweep(e2a, e2b, b2_right, a2, around(CX2, H2, 2), 4)
            sweep(e2b, e2a, b2_right, a2, around(CX2, H2, 1), 4)
            for j in range(CX2 + 2):
                spread = double(e2a[H2 - 1 + j, pl.ds(HY // 2, CY1)], CY1)
                low = H1 - 2 + 2 * j
                e1b[low] = e1b[low] + spread
                e1b[low + 1] = e1b[low + 1] + spread
            sweep(e1b, e1a, b1_right, a1, around(CX1, H1, 1), 2)
            for i in range(CX1):
                new = relaxed(e1a, b1[H1 + i], a1, H1 + i, 2)[1]
                spread = double(new[HY : HY + CY1], CY1)
                low = H0 + 2 * i
                xa[low, y0] = xa[low, y0] + spread
                xa[low + 1, y0] = xa[low + 1, y0] + spread
            made = copies(NEAR, s_x, fine(xa, W0))
            start(made)
            turn = s * VCYCLES + c

            @pl.when(turn == 0)
            def _():
                for copy in row_copies:
                    copy.wait()
                lane = lax.broadcasted_iota(jnp.int32, (8, NZ), 1)
                total = jnp.zeros((8, NZ), F32)
                for k in range(gx_count):
                    table = listed[...] if k == 0 else by_row[k - 1]
                    owned = jnp.where(lane // gy_count == gx, table, 0.0)
                    sender = lax.rem(gx + gx_count - k, gx_count)
                    shift = lax.rem((sender - gx + gx_count) * gy_count, NZ)
                    total = total + pltpu.roll(owned, shift, 1)
                sorted_ref[...] = total
                for copy in col_copies:
                    copy.start()

            @pl.when(turn == 1)
            def _():
                for copy in col_copies:
                    copy.wait()
                lane = lax.broadcasted_iota(jnp.int32, (8, NZ), 1)
                mine = lax.rem(lane, gy_count) == gy
                total = jnp.zeros((8, NZ), F32)
                for k in range(gy_count):
                    table = sorted_ref[...] if k == 0 else by_col[k - 1]
                    sender = lax.rem(gy + gy_count - k, gy_count)
                    shift = lax.rem(sender - gy + NZ, NZ)
                    total = total + pltpu.roll(jnp.where(mine, table, 0.0), shift, 1)
                place_wells(total, src_ref)
                start(src_copies)

            @pl.when(turn == 3)
            def _():
                finish(src_copies)

            finish(made)

            @pl.when(c == 0)
            def _():
                finish(bb_copies)
                for i in around(CX0, H0, 4):
                    bl[i] = bb[i]

            sweep(xa, xb, bb_right, a0, around(CX0, H0, 4), 1)
            sweep(xb, xa, bb_right, a0, around(CX0, H0, 3), 1)
            return inner

        lax.fori_loop(0, VCYCLES, cycle, 0)

        @pl.when(s < TSTEPS)
        def _():
            for i in around(CX0, H0, 2):
                dps[s, i] = xa[i]

        @pl.when(s == TSTEPS - 1)
        def _():
            final_ref[...] = xa[pl.ds(H0, CX0), y0]
            xa[...] = jnp.zeros(xa.shape, F32)

        @pl.when(s >= TSTEPS)
        def _():
            step = 2 * TSTEPS - 1 - s
            for i in range(CX0):
                ext = H0 + i
                adjoint, adjoints = neighbours(xa, None, ext)
                press, presses = neighbours(pp, 1 + step, ext)
                total = jnp.zeros((NY0, NZ), F32)
                for f in range(6):
                    total = total + a0[f, ext] * (press - presses[f]) * (adjoint - adjoints[f])
                hess_ref[i] = hess_ref[i] - 0.5 * dg0[i] * total[HY : HY + CY0]

        return carry

    lax.fori_loop(0, 2 * TSTEPS, solve, 0)


def local(
    log_perm,
    perturb,
    storage,
    base_press,
    well_rows,
    well_cells,
    well_counts,
    well_owner,
    well_start,
):
    gx_count = lax.axis_size("gx")
    gy_count = lax.axis_size("gy")
    ints = jnp.stack([well_cells, well_counts, well_owner[:, 0], well_start])
    ext0 = (NX0, NY0, NZ)
    ext1 = (NX1, NY1, NZ)
    ext2 = (NX2, NY2, NZ)
    core0 = (CX0, CY0, NZ)
    core1 = (CX1, CY1, NZ)
    core2 = (CX2, CY2, NZ)

    def vmem(*shape):
        return pltpu.VMEM(shape, F32)

    def sems(count):
        return pltpu.SemaphoreType.DMA((2, count))

    spec = pl.BlockSpec(memory_space=pltpu.VMEM)

    def body(*refs):
        kernel(gx_count, gy_count, *refs)

    return pl.pallas_call(
        body,
        out_shape=(
            jax.ShapeDtypeStruct(core0, F32),
            jax.ShapeDtypeStruct(core0, F32),
        ),
        in_specs=[spec] * 6,
        out_specs=(spec, spec),
        scratch_shapes=[
            vmem(2, *ext0),
            vmem(2, *ext1),
            vmem(2, *ext2),
            vmem(3, *ext0),
            vmem(*ext0),
            vmem(*ext0),
            vmem(*ext0),
            vmem(6, *ext0),
            vmem(*ext0),
            vmem(*core0),
            vmem(*core0),
            vmem(*ext1),
            vmem(*ext1),
            vmem(*ext1),
            vmem(6, *ext1),
            vmem(*core1),
            vmem(*core1),
            vmem(*core1),
            vmem(*ext2),
            vmem(*ext2),
            vmem(*ext2),
            vmem(6, *ext2),
            vmem(*core2),
            vmem(CY0, NZ),
            vmem(*ext0),
            vmem(TSTEPS, *ext0),
            vmem(8, NZ),
            vmem(gx_count - 1, 8, NZ),
            vmem(8, NZ),
            vmem(gy_count - 1, 8, NZ),
            vmem(TSTEPS, *ext0),
            sems(len(NEAR)),
            sems(len(NEAR)),
            sems(len(WIDE)),
            sems(len(NEAR)),
            sems(len(NEAR)),
            sems(len(NEAR)),
            sems(len(NEAR)),
            sems(len(WIDE)),
            sems(gx_count - 1),
            sems(gy_count - 1),
            sems(len(NEAR)),
        ],
        compiler_params=pltpu.CompilerParams(collective_id=0, has_side_effects=True),
    )(log_perm, perturb, storage, base_press, well_rows, ints)


def solution(mesh):
    return jax.shard_map(
        local,
        mesh=mesh,
        in_specs=(
            P("gx", "gy", None),
            P("gx", "gy", None),
            P("gx", "gy", None),
            P(None, "gx", "gy", None),
            P(("gx", "gy"), None),
            P(("gx", "gy")),
            P(("gx", "gy")),
            P(("gx", "gy"), None),
            P(("gx", "gy")),
        ),
        out_specs=(P("gx", "gy", None), P("gx", "gy", None)),
        check_vma=False,
    )
```

```python
import jax
import jax.numpy as jnp
from jax import lax
from jax.experimental import pallas as pl
from jax.experimental.pallas import tpu as pltpu
from jax.sharding import PartitionSpec as P

TSTEPS = 2
VCYCLES = 2
SAMPLES = 512
CAP = 2
OMEGA = 0.8

F32 = jnp.float32
MESH = pl.DeviceIdType.MESH

CX0, CY0, H0, W0 = 8, 32, 5, 5
CX1, CY1, H1, HY1 = 4, 16, 10, 16
CX2, CY2, H2 = 2, 8, 5
HY = 8
NX0, NY0 = CX0 + 2 * H0, CY0 + 2 * HY
NX1, NY1 = CX1 + 2 * H1, CY1 + 2 * HY1
NX2, NY2 = CX2 + 2 * H2, CY2 + 2 * HY
NZ = 128


def ordered(offsets):
    return sorted(offsets, key=lambda o: (o[1] == 0, -abs(o[0]), o))


NEAR = ordered([(dx, dy) for dx in (-1, 0, 1) for dy in (-1, 0, 1) if (dx, dy) != (0, 0)])
WIDE = ordered([(dx, dy) for dx in range(-3, 4) for dy in (-1, 0, 1) if (dx, dy) != (0, 0)])


def span_x(dx, core, halo, width):
    if dx > 0:
        return pl.ds(halo + core - width, width), pl.ds(halo - width, width)
    if dx < 0:
        return pl.ds(halo, width), pl.ds(halo + core, width)
    return pl.ds(halo, core), pl.ds(halo, core)


def span_y(dy, core, width, halo=HY):
    if dy > 0:
        return pl.ds(halo + core - width, width), pl.ds(halo - width, width)
    if dy < 0:
        return pl.ds(halo, width), pl.ds(halo + core, width)
    return pl.ds(halo, core), pl.ds(halo, core)


def strips(ref, core_x, halo, width, core_y):
    def at(dx, dy):
        if dx != 0 and dy != 0:
            deep, rows = width - 1, 4 * -(-(width - 1) // 4)
        else:
            deep, rows = width, 4 * -(-width // 4)
        sx, tx = span_x(dx, core_x, halo, deep)
        sy, ty = span_y(dy, core_y, rows)
        if len(ref.shape) == 4:
            return ref.at[:, sx, sy], ref.at[:, tx, ty]
        return ref.at[sx, sy], ref.at[tx, ty]

    return at


def packed(ref):
    first, count = H1 // 2, CX1 // 2

    def at(dx, dy):
        if abs(dx) < 3:
            sx, tx = pl.ds(first, count), pl.ds(first - count * dx, count)
        elif dx > 0:
            sx, tx = pl.ds(first + count - 1, 1), pl.ds(0, 1)
        else:
            sx, tx = pl.ds(first, 1), pl.ds(2 * first + count - 1, 1)
        sy, ty = span_y(dy, CY1, (12, 12, 8, 4)[abs(dx)], HY1)
        if len(ref.shape) == 4:
            return ref.at[:, sx, sy], ref.at[:, tx, ty]
        return ref.at[sx, sy], ref.at[tx, ty]

    return at


def even_layers(shape):
    return (lax.broadcasted_iota(jnp.int32, shape, len(shape) - 1) & 1) == 0


def unpacked(values):
    even = even_layers(values.shape)
    return (
        jnp.where(even, values, pltpu.roll(values, 1, 1)),
        jnp.where(even, pltpu.roll(values, NZ - 1, 1), values),
    )


def swap_pair(values, stride):
    lane = lax.broadcasted_iota(jnp.int32, values.shape, values.ndim - 1)
    axis = values.ndim - 1
    return jnp.where(
        (lane & stride) == 0,
        pltpu.roll(values, NZ - stride, axis),
        pltpu.roll(values, stride, axis),
    )


def list_wells(rows_ref, ints_ref, listed):
    wells = rows_ref.shape[0]
    lane = lax.broadcasted_iota(jnp.int32, (wells, NZ), 1).astype(F32)
    well = lax.broadcasted_iota(jnp.int32, (wells, NZ), 0).astype(F32)
    across = [
        jnp.broadcast_to(ints_ref[pl.ds(k, 1), :].astype(F32), (NZ, wells)) for k in range(4)
    ]
    cell, count, owner, begin = [jnp.transpose(values) for values in across]
    fields = [cell]
    span = SAMPLES // TSTEPS
    for step in range(TSTEPS):
        total = jnp.zeros((wells, NZ), F32)
        for first in range(step * span, (step + 1) * span, NZ):
            records = rows_ref[:, pl.ds(first, NZ)]
            total = total + jnp.where(lane + float(first) < count, records, 0.0)
        total = jnp.sum(total, axis=1, keepdims=True)
        fields.append(jnp.where(begin <= float(step), total, 0.0))
    earlier = jnp.logical_and(owner == across[2], lane < well)
    rank = jnp.sum(jnp.where(earlier, 1.0, 0.0), axis=1, keepdims=True)
    listed[...] = jnp.zeros(listed.shape, F32)
    for slot in range(CAP):
        hit = jnp.logical_and(owner == lane, rank == float(slot))
        for f, field in enumerate(fields):
            listed[pl.ds(3 * slot + f, 1), :] = jnp.sum(
                jnp.where(hit, field, 0.0), axis=0, keepdims=True
            )


def place_wells(table, src_ref):
    columns = CX0 * CY0
    column = lax.broadcasted_iota(jnp.int32, (columns, NZ), 0)
    layer = lax.broadcasted_iota(jnp.int32, (NZ, NZ), 0)
    placed = [None] * TSTEPS
    for slot in range(CAP):
        cell = table[3 * slot : 3 * slot + 1].astype(jnp.int32)
        here = column == cell // NZ
        deep = jnp.where(layer == lax.rem(cell, NZ), 1.0, 0.0)
        for step in range(TSTEPS):
            weight = table[3 * slot + 1 + step : 3 * slot + 2 + step]
            part = lax.dot_general(
                jnp.where(here, weight, 0.0),
                deep,
                (((1,), (1,)), ((), ())),
                precision=lax.Precision.HIGHEST,
                preferred_element_type=F32,
            )
            placed[step] = part if placed[step] is None else placed[step] + part
    for step in range(TSTEPS):
        src_ref[step, pl.ds(H0, CX0), pl.ds(HY, CY0)] = placed[step].reshape(CX0, CY0, NZ)


def kernel(
    gx_count,
    gy_count,
    log_ref,
    pert_ref,
    stor_ref,
    press_ref,
    rows_ref,
    ints_ref,
    hess_ref,
    final_ref,
    ms0,
    ms1,
    ms2,
    pks,
    pk,
    pp,
    xa,
    xb,
    bb,
    a0,
    dinv0,
    dg0,
    r0,
    b1,
    e1a,
    e1b,
    a1,
    dinv1,
    dg1,
    b2,
    e2a,
    e2b,
    a2,
    dinv2,
    pair,
    bl,
    dps,
    listed,
    by_row,
    sorted_ref,
    by_col,
    src_ref,
    s_ms0,
    s_ms1,
    s_pp,
    s_bb,
    s_x,
    s_b1,
    s_row,
    s_col,
    s_src,
):
    gx = lax.axis_index("gx")
    gy = lax.axis_index("gy")

    def exists(dx, dy):
        tx, ty = gx + dx, gy + dy
        ok = None
        for cond in (
            [tx >= 0] * (dx < 0) + [tx < gx_count] * (dx > 0)
            + [ty >= 0] * (dy < 0) + [ty < gy_count] * (dy > 0)
        ):
            ok = cond if ok is None else jnp.logical_and(ok, cond)
        return ok

    def copies(offsets, sems, views):
        made = []
        for index, (dx, dy) in enumerate(offsets):
            source, target = views(dx, dy)
            made.append(
                (
                    dx,
                    dy,
                    pltpu.make_async_remote_copy(
                        src_ref=source,
                        dst_ref=target,
                        send_sem=sems.at[0, index],
                        recv_sem=sems.at[1, index],
                        device_id=(gx + dx, gy + dy),
                        device_id_type=MESH,
                    ),
                )
            )
        return made

    def start(made):
        for dx, dy, copy in made:
            pl.when(exists(dx, dy))(copy.start)

    def finish(made):
        for dx, dy, copy in made:
            pl.when(exists(-dx, -dy))(copy.wait_recv)
        for dx, dy, copy in made:
            pl.when(exists(dx, dy))(copy.wait_send)

    def spread(table, slots, sems, peers):
        return [
            pltpu.make_async_remote_copy(
                src_ref=table,
                dst_ref=slots.at[k],
                send_sem=sems.at[0, k],
                recv_sem=sems.at[1, k],
                device_id=peer,
                device_id_type=MESH,
            )
            for k, peer in enumerate(peers)
        ]

    def fine(ref, width):
        return strips(ref, CX0, H0, width, CY0)

    def halve(first, second, size, stride):
        pair[pl.ds(0, 2 * size), :] = first + second
        summed = pair[pl.ds(0, size, stride=2), :] + pair[pl.ds(1, size, stride=2), :]
        return 0.125 * (summed + swap_pair(summed, stride))

    def double(values, size):
        pair[pl.ds(0, size, stride=2), :] = values
        pair[pl.ds(1, size, stride=2), :] = values
        return pair[pl.ds(0, 2 * size), :]

    y0, y1 = pl.ds(HY, CY0), pl.ds(HY1, CY1)
    even = even_layers((CY1, NZ))

    for ref in (ms0, pk, pks, pp, xa, xb, bb, b1, e1a, e1b, b2, e2a, e2b, a0, a1, a2, bl, dps, src_ref, dinv0):
        ref[...] = jnp.zeros(ref.shape, F32)
    hess_ref[...] = jnp.zeros(hess_ref.shape, F32)
    for i in range(CX0):
        ms0[0, H0 + i, y0] = log_ref[i]
        ms0[1, H0 + i, y0] = stor_ref[i]
        pp[0, H0 + i, y0] = pert_ref[i]
        pp[1, H0 + i, y0] = press_ref[0, i]
        pp[2, H0 + i, y0] = press_ref[1, i]
    for f, ref in enumerate((log_ref, stor_ref)):
        means = [halve(ref[2 * i], ref[2 * i + 1], CY1, 1) for i in range(CX1)]
        for p in range(CX1 // 2):
            pks[f, H1 // 2 + p, y1] = jnp.where(even, means[2 * p], means[2 * p + 1])

    row_peers = [(lax.rem(gx + k, gx_count), gy) for k in range(1, gx_count)]
    col_peers = [(gx, lax.rem(gy + k, gy_count)) for k in range(1, gy_count)]

    barrier = pltpu.get_barrier_semaphore()
    for peer in row_peers + col_peers:
        pl.semaphore_signal(barrier, inc=1, device_id=peer, device_id_type=MESH)
    for dx, dy in WIDE:
        if dx != 0 and dy != 0:

            @pl.when(exists(dx, dy))
            def _():
                pl.semaphore_signal(
                    barrier, inc=1, device_id=(gx + dx, gy + dy), device_id_type=MESH
                )

    beside_x = jnp.minimum(gx, 3) + jnp.minimum(gx_count - 1 - gx, 3)
    beside_y = jnp.minimum(gy, 1) + jnp.minimum(gy_count - 1 - gy, 1)
    pl.semaphore_wait(barrier, beside_x * beside_y + gx_count - 1 + gy_count - 1)

    setup = [
        copies(NEAR, s_ms0, fine(ms0, W0)),
        copies(WIDE, s_ms1, packed(pks)),
        copies(NEAR, s_pp, fine(pp, 3)),
    ]
    for made in setup:
        start(made)
    list_wells(rows_ref, ints_ref, listed)
    row_copies = spread(listed, by_row, s_row, row_peers)
    for copy in row_copies:
        copy.start()
    for made in setup:
        finish(made)
    for f in range(2):
        for p in range(NX1 // 2):
            ms1[f, 2 * p], ms1[f, 2 * p + 1] = unpacked(pks[f, p])
        for j in range(NX2):
            ms2[f, j] = halve(ms1[f, 2 * j], ms1[f, 2 * j + 1], NY2, 2)

    def coefficients(ms, a, dinv, dg, factor, rows, core, halo, core_y, stride):
        ny = ms.shape[2]
        halo_y = (ny - core_y) // 2
        row = lax.broadcasted_iota(jnp.int32, (ny, NZ), 0) - halo_y + gy * core_y
        inside_y = jnp.logical_and(row >= 0, row < gy_count * core_y)
        lane = lax.broadcasted_iota(jnp.int32, (ny, NZ), 1)
        for i in rows:
            m = ms[0, i]
            total = ms[1, i]
            faces = []
            for other in (
                ms[0, i - 1],
                ms[0, i + 1],
                pltpu.roll(m, 1, 0),
                pltpu.roll(m, ny - 1, 0),
                pltpu.roll(m, stride, 1),
                pltpu.roll(m, NZ - stride, 1),
            ):
                faces.append(factor * jnp.exp(0.5 * (m + other)))
            faces[4] = jnp.where(lane >= stride, faces[4], 0.0)
            faces[5] = jnp.where(lane < NZ - stride, faces[5], 0.0)
            for face in faces:
                total = total + face
            place = gx * core + (i - halo)
            inside_x = jnp.logical_and(place >= 0, place < gx_count * core)
            scale = jnp.where(jnp.logical_and(inside_y, inside_x), OMEGA / total, 0.0)
            for f in range(6):
                a[f, i] = faces[f] * scale
            dinv[i] = scale
            if dg is not None:
                dg[i] = total * (1.0 / OMEGA)

    coefficients(ms0, a0, dinv0, dg0, 1.0, range(1, NX0 - 1), CX0, H0, CY0, 1)
    coefficients(ms1, a1, dinv1, dg1, 0.25, range(1, NX1 - 1), CX1, H1, CY1, 2)
    coefficients(ms2, a2, dinv2, None, 0.0625, range(1, NX2 - 1), CX2, H2, CY2, 4)

    def relaxed(src, right, a, i, stride):
        ny = src.shape[0 if src.ndim == 2 else 1]
        c = src[i]
        new = (1.0 - OMEGA) * c + right
        new = new + a[0, i] * src[i - 1] + a[1, i] * src[i + 1]
        new = new + a[2, i] * pltpu.roll(c, 1, 0) + a[3, i] * pltpu.roll(c, ny - 1, 0)
        new = new + a[4, i] * pltpu.roll(c, stride, 1) + a[5, i] * pltpu.roll(c, NZ - stride, 1)
        return c, new

    def sweep(src, dst, right, a, rows, stride):
        for i in rows:
            dst[i] = relaxed(src, right(i), a, i, stride)[1]

    def around(core, halo, extra):
        return range(halo - extra, halo + core + extra)

    bb_right = lambda i: bl[i]
    b1_right = lambda i: b1[i]
    b2_right = lambda i: b2[i]

    def neighbours(ref, lead, i):
        c = ref[lead, i] if lead is not None else ref[i]
        down = ref[lead, i - 1] if lead is not None else ref[i - 1]
        up = ref[lead, i + 1] if lead is not None else ref[i + 1]
        ny = c.shape[0]
        return c, (
            down,
            up,
            pltpu.roll(c, 1, 0),
            pltpu.roll(c, ny - 1, 0),
            pltpu.roll(c, 1, 1),
            pltpu.roll(c, NZ - 1, 1),
        )

    col_copies = spread(sorted_ref, by_col, s_col, col_peers)
    src_copies = copies(NEAR, s_src, fine(src_ref, 2))

    def solve(s, carry):
        @pl.when(s < TSTEPS)
        def _():
            for i in around(CX0, H0, 2):
                change, changes = neighbours(pp, 0, i)
                press, presses = neighbours(pp, 1 + s, i)
                total = dinv0[i] * (ms0[1, i] * xa[i])
                for f in range(6):
                    total = total - a0[f, i] * (0.5 * (change + changes[f])) * (press - presses[f])
                bl[i] = total

        @pl.when(s >= TSTEPS)
        def _():
            step = 2 * TSTEPS - 1 - s
            for i in around(CX0, H0, 2):
                bl[i] = dinv0[i] * (ms0[1, i] * xa[i] + src_ref[step, i] * dps[step, i])

        for i in around(CX0, H0, 0):
            bb[i, y0] = bl[i, y0]
        xa[...] = jnp.zeros(xa.shape, F32)
        bb_copies = copies(NEAR, s_bb, fine(bb, W0 - 1))

        def cycle(c, inner):
            turn = s * VCYCLES + c
            half = lax.rem(turn, 2)
            sweep(xa, xb, bb_right, a0, around(CX0, H0, 2), 1)
            sweep(xb, xa, bb_right, a0, around(CX0, H0, 1), 1)
            for i in range(CX0):
                old, new = relaxed(xa, bb_right(H0 + i), a0, H0 + i, 1)
                r0[i] = ((new - old) * dg0[H0 + i])[HY : HY + CY0]
            sides = [
                dinv1[H1 + i, y1] * halve(r0[2 * i], r0[2 * i + 1], CY1, 1) for i in range(CX1)
            ]
            for p in range(CX1 // 2):
                pk[half, H1 // 2 + p, y1] = jnp.where(even, sides[2 * p], sides[2 * p + 1])
            made = copies(WIDE, s_b1.at[half], packed(pk.at[half]))
            start(made)

            @pl.when(c == 0)
            def _():
                start(bb_copies)

            finish(made)
            for p in range(NX1 // 2):
                b1[2 * p], b1[2 * p + 1] = unpacked(pk[half, p])
            sweep(b1, e1b, b1_right, a1, around(CX1, H1, 9), 2)
            for j in range(1, NX2 - 1):
                pairs = []
                for i in (2 * j, 2 * j + 1):
                    old, new = relaxed(e1b, b1[i], a1, i, 2)
                    pairs.append((new - old) * dg1[i])
                b2[j] = dinv2[j] * halve(pairs[0], pairs[1], NY2, 2)
            sweep(b2, e2a, b2_right, a2, around(CX2, H2, 3), 4)
            sweep(e2a, e2b, b2_right, a2, around(CX2, H2, 2), 4)
            sweep(e2b, e2a, b2_right, a2, around(CX2, H2, 1), 4)
            for j in range(CX2 + 2):
                spread = double(e2a[H2 - 1 + j], NY2)
                low = H1 - 2 + 2 * j
                e1b[low] = e1b[low] + spread
                e1b[low + 1] = e1b[low + 1] + spread
            sweep(e1b, e1a, b1_right, a1, around(CX1, H1, 1), 2)
            for i in range(CX1):
                new = relaxed(e1a, b1[H1 + i], a1, H1 + i, 2)[1]
                spread = double(new[HY1 : HY1 + CY1], CY1)
                low = H0 + 2 * i
                xa[low, y0] = xa[low, y0] + spread
                xa[low + 1, y0] = xa[low + 1, y0] + spread
            made = copies(NEAR, s_x, fine(xa, W0))
            start(made)

            @pl.when(turn == 0)
            def _():
                for copy in row_copies:
                    copy.wait()
                lane = lax.broadcasted_iota(jnp.int32, (8, NZ), 1)
                total = jnp.zeros((8, NZ), F32)
                for k in range(gx_count):
                    table = listed[...] if k == 0 else by_row[k - 1]
                    owned = jnp.where(lane // gy_count == gx, table, 0.0)
                    sender = lax.rem(gx + gx_count - k, gx_count)
                    shift = lax.rem((sender - gx + gx_count) * gy_count, NZ)
                    total = total + pltpu.roll(owned, shift, 1)
                sorted_ref[...] = total
                for copy in col_copies:
                    copy.start()

            @pl.when(turn == 1)
            def _():
                for copy in col_copies:
                    copy.wait()
                lane = lax.broadcasted_iota(jnp.int32, (8, NZ), 1)
                mine = lax.rem(lane, gy_count) == gy
                total = jnp.zeros((8, NZ), F32)
                for k in range(gy_count):
                    table = sorted_ref[...] if k == 0 else by_col[k - 1]
                    sender = lax.rem(gy + gy_count - k, gy_count)
                    shift = lax.rem(sender - gy + NZ, NZ)
                    total = total + pltpu.roll(jnp.where(mine, table, 0.0), shift, 1)
                place_wells(total, src_ref)
                start(src_copies)

            @pl.when(turn == 3)
            def _():
                finish(src_copies)

            finish(made)

            @pl.when(c == 0)
            def _():
                finish(bb_copies)
                for i in around(CX0, H0, 4):
                    bl[i] = bb[i]

            sweep(xa, xb, bb_right, a0, around(CX0, H0, 4), 1)
            sweep(xb, xa, bb_right, a0, around(CX0, H0, 3), 1)
            return inner

        lax.fori_loop(0, VCYCLES, cycle, 0)

        @pl.when(s < TSTEPS)
        def _():
            for i in around(CX0, H0, 2):
                dps[s, i] = xa[i]

        @pl.when(s == TSTEPS - 1)
        def _():
            final_ref[...] = xa[pl.ds(H0, CX0), y0]
            xa[...] = jnp.zeros(xa.shape, F32)

        @pl.when(s >= TSTEPS)
        def _():
            step = 2 * TSTEPS - 1 - s
            for i in range(CX0):
                ext = H0 + i
                adjoint, adjoints = neighbours(xa, None, ext)
                press, presses = neighbours(pp, 1 + step, ext)
                total = jnp.zeros((NY0, NZ), F32)
                for f in range(6):
                    total = total + a0[f, ext] * (press - presses[f]) * (adjoint - adjoints[f])
                hess_ref[i] = hess_ref[i] - (0.5 * dg0[ext] * total)[HY : HY + CY0]

        return carry

    lax.fori_loop(0, 2 * TSTEPS, solve, 0)


def local(
    log_perm,
    perturb,
    storage,
    base_press,
    well_rows,
    well_cells,
    well_counts,
    well_owner,
    well_start,
):
    gx_count = lax.axis_size("gx")
    gy_count = lax.axis_size("gy")
    ints = jnp.stack([well_cells, well_counts, well_owner[:, 0], well_start])
    ext0 = (NX0, NY0, NZ)
    ext1 = (NX1, NY1, NZ)
    ext2 = (NX2, NY2, NZ)
    core0 = (CX0, CY0, NZ)

    def vmem(*shape):
        return pltpu.VMEM(shape, F32)

    def sems(count):
        return pltpu.SemaphoreType.DMA((2, count))

    spec = pl.BlockSpec(memory_space=pltpu.VMEM)

    def body(*refs):
        kernel(gx_count, gy_count, *refs)

    return pl.pallas_call(
        body,
        out_shape=(
            jax.ShapeDtypeStruct(core0, F32),
            jax.ShapeDtypeStruct(core0, F32),
        ),
        in_specs=[spec] * 6,
        out_specs=(spec, spec),
        scratch_shapes=[
            vmem(2, *ext0),
            vmem(2, *ext1),
            vmem(2, *ext2),
            vmem(2, NX1 // 2, NY1, NZ),
            vmem(2, NX1 // 2, NY1, NZ),
            vmem(3, *ext0),
            vmem(*ext0),
            vmem(*ext0),
            vmem(*ext0),
            vmem(6, *ext0),
            vmem(*ext0),
            vmem(*ext0),
            vmem(*core0),
            vmem(*ext1),
            vmem(*ext1),
            vmem(*ext1),
            vmem(6, *ext1),
            vmem(*ext1),
            vmem(*ext1),
            vmem(*ext2),
            vmem(*ext2),
            vmem(*ext2),
            vmem(6, *ext2),
            vmem(*ext2),
            vmem(NY1, NZ),
            vmem(*ext0),
            vmem(TSTEPS, *ext0),
            vmem(8, NZ),
            vmem(gx_count - 1, 8, NZ),
            vmem(8, NZ),
            vmem(gy_count - 1, 8, NZ),
            vmem(TSTEPS, *ext0),
            sems(len(NEAR)),
            sems(len(WIDE)),
            sems(len(NEAR)),
            sems(len(NEAR)),
            sems(len(NEAR)),
            pltpu.SemaphoreType.DMA((2, 2, len(WIDE))),
            sems(gx_count - 1),
            sems(gy_count - 1),
            sems(len(NEAR)),
        ],
        compiler_params=pltpu.CompilerParams(collective_id=0, has_side_effects=True),
    )(log_perm, perturb, storage, base_press, well_rows, ints)


def solution(mesh):
    return jax.shard_map(
        local,
        mesh=mesh,
        in_specs=(
            P("gx", "gy", None),
            P("gx", "gy", None),
            P("gx", "gy", None),
            P(None, "gx", "gy", None),
            P(("gx", "gy"), None),
            P(("gx", "gy")),
            P(("gx", "gy")),
            P(("gx", "gy"), None),
            P(("gx", "gy")),
        ),
        out_specs=(P("gx", "gy", None), P("gx", "gy", None)),
        check_vma=False,
    )
```

```python
import jax
import jax.numpy as jnp
from jax import lax
from jax.experimental import pallas as pl
from jax.experimental.pallas import tpu as pltpu
from jax.sharding import PartitionSpec as P

TSTEPS = 2
VCYCLES = 2
SAMPLES = 512
CAP = 2
OMEGA = 0.8

F32 = jnp.float32
MESH = pl.DeviceIdType.MESH

CX0, CY0, H0, W0 = 8, 32, 5, 5
CX1, CY1, H1, HY1 = 4, 16, 10, 16
CX2, CY2, H2 = 2, 8, 5
HY = 8
NX0, NY0 = CX0 + 2 * H0, CY0 + 2 * HY
NX1, NY1 = CX1 + 2 * H1, CY1 + 2 * HY1
NX2, NY2 = CX2 + 2 * H2, CY2 + 2 * HY
NZ = 128


def ordered(offsets):
    return sorted(offsets, key=lambda o: (o[1] == 0, -abs(o[0]), o))


NEAR = ordered([(dx, dy) for dx in (-1, 0, 1) for dy in (-1, 0, 1) if (dx, dy) != (0, 0)])
WIDE = ordered([(dx, dy) for dx in range(-3, 4) for dy in (-1, 0, 1) if (dx, dy) != (0, 0)])


def span_x(dx, core, halo, width):
    if dx > 0:
        return pl.ds(halo + core - width, width), pl.ds(halo - width, width)
    if dx < 0:
        return pl.ds(halo, width), pl.ds(halo + core, width)
    return pl.ds(halo, core), pl.ds(halo, core)


def span_y(dy, core, width, halo=HY):
    if dy > 0:
        return pl.ds(halo + core - width, width), pl.ds(halo - width, width)
    if dy < 0:
        return pl.ds(halo, width), pl.ds(halo + core, width)
    return pl.ds(halo, core), pl.ds(halo, core)


def strips(ref, core_x, halo, width, core_y):
    def at(dx, dy):
        if dx != 0 and dy != 0:
            deep, rows = width - 1, 4 * -(-(width - 1) // 4)
        else:
            deep, rows = width, 4 * -(-width // 4)
        sx, tx = span_x(dx, core_x, halo, deep)
        sy, ty = span_y(dy, core_y, rows)
        if len(ref.shape) == 4:
            return ref.at[:, sx, sy], ref.at[:, tx, ty]
        return ref.at[sx, sy], ref.at[tx, ty]

    return at


def packed(ref):
    first, count = H1 // 2, CX1 // 2

    def at(dx, dy):
        if abs(dx) < 3:
            sx, tx = pl.ds(first, count), pl.ds(first - count * dx, count)
        elif dx > 0:
            sx, tx = pl.ds(first + count - 1, 1), pl.ds(0, 1)
        else:
            sx, tx = pl.ds(first, 1), pl.ds(2 * first + count - 1, 1)
        sy, ty = span_y(dy, CY1, (12, 12, 8, 4)[abs(dx)], HY1)
        if len(ref.shape) == 4:
            return ref.at[:, sx, sy], ref.at[:, tx, ty]
        return ref.at[sx, sy], ref.at[tx, ty]

    return at


def even_layers(shape):
    return (lax.broadcasted_iota(jnp.int32, shape, len(shape) - 1) & 1) == 0


def unpacked(values):
    even = even_layers(values.shape)
    return (
        jnp.where(even, values, pltpu.roll(values, 1, 1)),
        jnp.where(even, pltpu.roll(values, NZ - 1, 1), values),
    )


def swap_pair(values, stride):
    lane = lax.broadcasted_iota(jnp.int32, values.shape, values.ndim - 1)
    axis = values.ndim - 1
    return jnp.where(
        (lane & stride) == 0,
        pltpu.roll(values, NZ - stride, axis),
        pltpu.roll(values, stride, axis),
    )


def list_wells(rows_ref, ints_ref, listed):
    wells = rows_ref.shape[0]
    lane = lax.broadcasted_iota(jnp.int32, (wells, NZ), 1).astype(F32)
    well = lax.broadcasted_iota(jnp.int32, (wells, NZ), 0).astype(F32)
    across = [
        jnp.broadcast_to(ints_ref[pl.ds(k, 1), :].astype(F32), (NZ, wells)) for k in range(4)
    ]
    cell, count, owner, begin = [jnp.transpose(values) for values in across]
    fields = [cell]
    span = SAMPLES // TSTEPS
    for step in range(TSTEPS):
        total = jnp.zeros((wells, NZ), F32)
        for first in range(step * span, (step + 1) * span, NZ):
            records = rows_ref[:, pl.ds(first, NZ)]
            total = total + jnp.where(lane + float(first) < count, records, 0.0)
        total = jnp.sum(total, axis=1, keepdims=True)
        fields.append(jnp.where(begin <= float(step), total, 0.0))
    earlier = jnp.logical_and(owner == across[2], lane < well)
    rank = jnp.sum(jnp.where(earlier, 1.0, 0.0), axis=1, keepdims=True)
    listed[...] = jnp.zeros(listed.shape, F32)
    for slot in range(CAP):
        hit = jnp.logical_and(owner == lane, rank == float(slot))
        for f, field in enumerate(fields):
            listed[pl.ds(3 * slot + f, 1), :] = jnp.sum(
                jnp.where(hit, field, 0.0), axis=0, keepdims=True
            )


def place_wells(table, src_ref):
    columns = CX0 * CY0
    column = lax.broadcasted_iota(jnp.int32, (columns, NZ), 0)
    layer = lax.broadcasted_iota(jnp.int32, (NZ, NZ), 0)
    placed = [None] * TSTEPS
    for slot in range(CAP):
        cell = table[3 * slot : 3 * slot + 1].astype(jnp.int32)
        here = column == cell // NZ
        deep = jnp.where(layer == lax.rem(cell, NZ), 1.0, 0.0)
        for step in range(TSTEPS):
            weight = table[3 * slot + 1 + step : 3 * slot + 2 + step]
            part = lax.dot_general(
                jnp.where(here, weight, 0.0),
                deep,
                (((1,), (1,)), ((), ())),
                precision=lax.Precision.HIGHEST,
                preferred_element_type=F32,
            )
            placed[step] = part if placed[step] is None else placed[step] + part
    for step in range(TSTEPS):
        src_ref[step, pl.ds(H0, CX0), pl.ds(HY, CY0)] = placed[step].reshape(CX0, CY0, NZ)


def kernel(
    gx_count,
    gy_count,
    log_ref,
    pert_ref,
    stor_ref,
    press_ref,
    rows_ref,
    ints_ref,
    hess_ref,
    final_ref,
    ms0,
    ms1,
    ms2,
    pks,
    pk,
    pp,
    xa,
    xb,
    bb,
    a0,
    dinv0,
    dg0,
    r0,
    b1,
    e1a,
    e1b,
    a1,
    dinv1,
    dg1,
    b2,
    e2a,
    e2b,
    a2,
    dinv2,
    pair,
    bl,
    dps,
    listed,
    by_row,
    sorted_ref,
    by_col,
    src_ref,
    s_ms0,
    s_ms1,
    s_pp,
    s_bb,
    s_x,
    s_b1,
    s_row,
    s_col,
    s_src,
):
    gx = lax.axis_index("gx")
    gy = lax.axis_index("gy")

    def exists(dx, dy):
        tx, ty = gx + dx, gy + dy
        ok = None
        for cond in (
            [tx >= 0] * (dx < 0) + [tx < gx_count] * (dx > 0)
            + [ty >= 0] * (dy < 0) + [ty < gy_count] * (dy > 0)
        ):
            ok = cond if ok is None else jnp.logical_and(ok, cond)
        return ok

    def copies(offsets, sems, views):
        made = []
        for index, (dx, dy) in enumerate(offsets):
            source, target = views(dx, dy)
            made.append(
                (
                    dx,
                    dy,
                    pltpu.make_async_remote_copy(
                        src_ref=source,
                        dst_ref=target,
                        send_sem=sems.at[0, index],
                        recv_sem=sems.at[1, index],
                        device_id=(gx + dx, gy + dy),
                        device_id_type=MESH,
                    ),
                )
            )
        return made

    def start(made):
        for dx, dy, copy in made:
            pl.when(exists(dx, dy))(copy.start)

    def finish(made):
        for dx, dy, copy in made:
            pl.when(exists(-dx, -dy))(copy.wait_recv)
        for dx, dy, copy in made:
            pl.when(exists(dx, dy))(copy.wait_send)

    def spread(table, slots, sems, peers):
        return [
            pltpu.make_async_remote_copy(
                src_ref=table,
                dst_ref=slots.at[k],
                send_sem=sems.at[0, k],
                recv_sem=sems.at[1, k],
                device_id=peer,
                device_id_type=MESH,
            )
            for k, peer in enumerate(peers)
        ]

    def fine(ref, width):
        return strips(ref, CX0, H0, width, CY0)

    def halve(first, second, size, stride):
        pair[pl.ds(0, 2 * size), :] = first + second
        summed = pair[pl.ds(0, size, stride=2), :] + pair[pl.ds(1, size, stride=2), :]
        return 0.125 * (summed + swap_pair(summed, stride))

    def double(values, size):
        pair[pl.ds(0, size, stride=2), :] = values
        pair[pl.ds(1, size, stride=2), :] = values
        return pair[pl.ds(0, 2 * size), :]

    y0, y1 = pl.ds(HY, CY0), pl.ds(HY1, CY1)
    even = even_layers((CY1, NZ))

    for ref in (ms0, pk, pks, pp, xa, xb, bb, b1, e1a, e1b, b2, e2a, e2b, a0, a1, a2, bl, dps, src_ref, dinv0):
        ref[...] = jnp.zeros(ref.shape, F32)
    hess_ref[...] = jnp.zeros(hess_ref.shape, F32)
    for i in range(CX0):
        ms0[0, H0 + i, y0] = log_ref[i]
        ms0[1, H0 + i, y0] = stor_ref[i]
        pp[0, H0 + i, y0] = pert_ref[i]
        pp[1, H0 + i, y0] = press_ref[0, i]
        pp[2, H0 + i, y0] = press_ref[1, i]
    for f, ref in enumerate((log_ref, stor_ref)):
        means = [halve(ref[2 * i], ref[2 * i + 1], CY1, 1) for i in range(CX1)]
        for p in range(CX1 // 2):
            pks[f, H1 // 2 + p, y1] = jnp.where(even, means[2 * p], means[2 * p + 1])

    row_peers = [(lax.rem(gx + k, gx_count), gy) for k in range(1, gx_count)]
    col_peers = [(gx, lax.rem(gy + k, gy_count)) for k in range(1, gy_count)]

    barrier = pltpu.get_barrier_semaphore()
    for peer in row_peers + col_peers:
        pl.semaphore_signal(barrier, inc=1, device_id=peer, device_id_type=MESH)
    for dx, dy in WIDE:
        if dx != 0 and dy != 0:

            @pl.when(exists(dx, dy))
            def _():
                pl.semaphore_signal(
                    barrier, inc=1, device_id=(gx + dx, gy + dy), device_id_type=MESH
                )

    beside_x = jnp.minimum(gx, 3) + jnp.minimum(gx_count - 1 - gx, 3)
    beside_y = jnp.minimum(gy, 1) + jnp.minimum(gy_count - 1 - gy, 1)
    pl.semaphore_wait(barrier, beside_x * beside_y + gx_count - 1 + gy_count - 1)

    setup = [
        copies(NEAR, s_ms0, fine(ms0, W0)),
        copies(WIDE, s_ms1, packed(pks)),
        copies(NEAR, s_pp, fine(pp, 3)),
    ]
    for made in setup:
        start(made)
    list_wells(rows_ref, ints_ref, listed)
    row_copies = spread(listed, by_row, s_row, row_peers)
    for copy in row_copies:
        copy.start()
    def coefficients(ms, a, dinv, dg, factor, rows, core, halo, core_y, stride):
        ny = ms.shape[2]
        halo_y = (ny - core_y) // 2
        row = lax.broadcasted_iota(jnp.int32, (ny, NZ), 0) - halo_y + gy * core_y
        inside_y = jnp.logical_and(row >= 0, row < gy_count * core_y)
        lane = lax.broadcasted_iota(jnp.int32, (ny, NZ), 1)
        for i in rows:
            m = ms[0, i]
            total = ms[1, i]
            faces = []
            for other in (
                ms[0, i - 1],
                ms[0, i + 1],
                pltpu.roll(m, 1, 0),
                pltpu.roll(m, ny - 1, 0),
                pltpu.roll(m, stride, 1),
                pltpu.roll(m, NZ - stride, 1),
            ):
                faces.append(factor * jnp.exp(0.5 * (m + other)))
            faces[4] = jnp.where(lane >= stride, faces[4], 0.0)
            faces[5] = jnp.where(lane < NZ - stride, faces[5], 0.0)
            for face in faces:
                total = total + face
            place = gx * core + (i - halo)
            inside_x = jnp.logical_and(place >= 0, place < gx_count * core)
            scale = jnp.where(jnp.logical_and(inside_y, inside_x), OMEGA / total, 0.0)
            for f in range(6):
                a[f, i] = faces[f] * scale
            dinv[i] = scale
            if dg is not None:
                dg[i] = total * (1.0 / OMEGA)

    finish(setup[0])
    coefficients(ms0, a0, dinv0, dg0, 1.0, range(1, NX0 - 1), CX0, H0, CY0, 1)
    finish(setup[1])
    for f in range(2):
        for p in range(NX1 // 2):
            ms1[f, 2 * p], ms1[f, 2 * p + 1] = unpacked(pks[f, p])
        for j in range(NX2):
            ms2[f, j] = halve(ms1[f, 2 * j], ms1[f, 2 * j + 1], NY2, 2)
    coefficients(ms1, a1, dinv1, dg1, 0.25, range(1, NX1 - 1), CX1, H1, CY1, 2)
    coefficients(ms2, a2, dinv2, None, 0.0625, range(1, NX2 - 1), CX2, H2, CY2, 4)
    finish(setup[2])

    def relaxed(src, right, a, i, stride):
        ny = src.shape[0 if src.ndim == 2 else 1]
        c = src[i]
        new = (1.0 - OMEGA) * c + right
        new = new + a[0, i] * src[i - 1] + a[1, i] * src[i + 1]
        new = new + a[2, i] * pltpu.roll(c, 1, 0) + a[3, i] * pltpu.roll(c, ny - 1, 0)
        new = new + a[4, i] * pltpu.roll(c, stride, 1) + a[5, i] * pltpu.roll(c, NZ - stride, 1)
        return c, new

    def sweep(src, dst, right, a, rows, stride):
        for i in rows:
            dst[i] = relaxed(src, right(i), a, i, stride)[1]

    def around(core, halo, extra):
        return range(halo - extra, halo + core + extra)

    bb_right = lambda i: bl[i]
    b1_right = lambda i: b1[i]
    b2_right = lambda i: b2[i]

    def neighbours(ref, lead, i):
        c = ref[lead, i] if lead is not None else ref[i]
        down = ref[lead, i - 1] if lead is not None else ref[i - 1]
        up = ref[lead, i + 1] if lead is not None else ref[i + 1]
        ny = c.shape[0]
        return c, (
            down,
            up,
            pltpu.roll(c, 1, 0),
            pltpu.roll(c, ny - 1, 0),
            pltpu.roll(c, 1, 1),
            pltpu.roll(c, NZ - 1, 1),
        )

    col_copies = spread(sorted_ref, by_col, s_col, col_peers)
    src_copies = copies(NEAR, s_src, fine(src_ref, 2))

    def solve(s, carry):
        @pl.when(s < TSTEPS)
        def _():
            for i in around(CX0, H0, 2):
                change, changes = neighbours(pp, 0, i)
                press, presses = neighbours(pp, 1 + s, i)
                total = dinv0[i] * (ms0[1, i] * xa[i])
                for f in range(6):
                    total = total - a0[f, i] * (0.5 * (change + changes[f])) * (press - presses[f])
                bl[i] = total

        @pl.when(s >= TSTEPS)
        def _():
            step = 2 * TSTEPS - 1 - s
            for i in around(CX0, H0, 2):
                bl[i] = dinv0[i] * (ms0[1, i] * xa[i] + src_ref[step, i] * dps[step, i])

        for i in around(CX0, H0, 0):
            bb[i, y0] = bl[i, y0]
        xa[...] = jnp.zeros(xa.shape, F32)
        bb_copies = copies(NEAR, s_bb, fine(bb, W0 - 1))

        def cycle(c, inner):
            turn = s * VCYCLES + c
            half = lax.rem(turn, 2)
            @pl.when(c == 0)
            def _():
                for i in around(CX0, H0, 2):
                    xb[i] = bl[i]

            @pl.when(c > 0)
            def _():
                sweep(xa, xb, bb_right, a0, around(CX0, H0, 2), 1)

            sweep(xb, xa, bb_right, a0, around(CX0, H0, 1), 1)
            for i in range(CX0):
                old, new = relaxed(xa, bb_right(H0 + i), a0, H0 + i, 1)
                r0[i] = ((new - old) * dg0[H0 + i])[HY : HY + CY0]
            sides = [
                dinv1[H1 + i, y1] * halve(r0[2 * i], r0[2 * i + 1], CY1, 1) for i in range(CX1)
            ]
            for p in range(CX1 // 2):
                pk[half, H1 // 2 + p, y1] = jnp.where(even, sides[2 * p], sides[2 * p + 1])
            made = copies(WIDE, s_b1.at[half], packed(pk.at[half]))
            start(made)

            @pl.when(c == 0)
            def _():
                start(bb_copies)

            finish(made)
            for p in range(NX1 // 2):
                b1[2 * p], b1[2 * p + 1] = unpacked(pk[half, p])
            sweep(b1, e1b, b1_right, a1, around(CX1, H1, 9), 2)
            for j in range(1, NX2 - 1):
                pairs = []
                for i in (2 * j, 2 * j + 1):
                    old, new = relaxed(e1b, b1[i], a1, i, 2)
                    pairs.append((new - old) * dg1[i])
                b2[j] = dinv2[j] * halve(pairs[0], pairs[1], NY2, 2)
            sweep(b2, e2a, b2_right, a2, around(CX2, H2, 3), 4)
            sweep(e2a, e2b, b2_right, a2, around(CX2, H2, 2), 4)
            sweep(e2b, e2a, b2_right, a2, around(CX2, H2, 1), 4)
            for j in range(CX2 + 2):
                spread = double(e2a[H2 - 1 + j], NY2)
                low = H1 - 2 + 2 * j
                e1b[low] = e1b[low] + spread
                e1b[low + 1] = e1b[low + 1] + spread
            sweep(e1b, e1a, b1_right, a1, around(CX1, H1, 1), 2)
            for i in range(CX1):
                new = relaxed(e1a, b1[H1 + i], a1, H1 + i, 2)[1]
                spread = double(new[HY1 : HY1 + CY1], CY1)
                low = H0 + 2 * i
                xa[low, y0] = xa[low, y0] + spread
                xa[low + 1, y0] = xa[low + 1, y0] + spread
            made = copies(NEAR, s_x, fine(xa, W0))
            start(made)

            @pl.when(turn == 0)
            def _():
                for copy in row_copies:
                    copy.wait()
                lane = lax.broadcasted_iota(jnp.int32, (8, NZ), 1)
                total = jnp.zeros((8, NZ), F32)
                for k in range(gx_count):
                    table = listed[...] if k == 0 else by_row[k - 1]
                    owned = jnp.where(lane // gy_count == gx, table, 0.0)
                    sender = lax.rem(gx + gx_count - k, gx_count)
                    shift = lax.rem((sender - gx + gx_count) * gy_count, NZ)
                    total = total + pltpu.roll(owned, shift, 1)
                sorted_ref[...] = total
                for copy in col_copies:
                    copy.start()

            @pl.when(turn == 1)
            def _():
                for copy in col_copies:
                    copy.wait()
                lane = lax.broadcasted_iota(jnp.int32, (8, NZ), 1)
                mine = lax.rem(lane, gy_count) == gy
                total = jnp.zeros((8, NZ), F32)
                for k in range(gy_count):
                    table = sorted_ref[...] if k == 0 else by_col[k - 1]
                    sender = lax.rem(gy + gy_count - k, gy_count)
                    shift = lax.rem(sender - gy + NZ, NZ)
                    total = total + pltpu.roll(jnp.where(mine, table, 0.0), shift, 1)
                place_wells(total, src_ref)
                start(src_copies)

            @pl.when(turn == 3)
            def _():
                finish(src_copies)

            finish(made)

            @pl.when(c == 0)
            def _():
                finish(bb_copies)
                for i in around(CX0, H0, 4):
                    bl[i] = bb[i]

            sweep(xa, xb, bb_right, a0, around(CX0, H0, 4), 1)
            sweep(xb, xa, bb_right, a0, around(CX0, H0, 3), 1)
            return inner

        lax.fori_loop(0, VCYCLES, cycle, 0)

        @pl.when(s < TSTEPS)
        def _():
            for i in around(CX0, H0, 2):
                dps[s, i] = xa[i]

        @pl.when(s == TSTEPS - 1)
        def _():
            final_ref[...] = xa[pl.ds(H0, CX0), y0]
            xa[...] = jnp.zeros(xa.shape, F32)

        @pl.when(s >= TSTEPS)
        def _():
            step = 2 * TSTEPS - 1 - s
            for i in range(CX0):
                ext = H0 + i
                adjoint, adjoints = neighbours(xa, None, ext)
                press, presses = neighbours(pp, 1 + step, ext)
                total = jnp.zeros((NY0, NZ), F32)
                for f in range(6):
                    total = total + a0[f, ext] * (press - presses[f]) * (adjoint - adjoints[f])
                hess_ref[i] = hess_ref[i] - (0.5 * dg0[ext] * total)[HY : HY + CY0]

        return carry

    lax.fori_loop(0, 2 * TSTEPS, solve, 0)


def local(
    log_perm,
    perturb,
    storage,
    base_press,
    well_rows,
    well_cells,
    well_counts,
    well_owner,
    well_start,
):
    gx_count = lax.axis_size("gx")
    gy_count = lax.axis_size("gy")
    ints = jnp.stack([well_cells, well_counts, well_owner[:, 0], well_start])
    ext0 = (NX0, NY0, NZ)
    ext1 = (NX1, NY1, NZ)
    ext2 = (NX2, NY2, NZ)
    core0 = (CX0, CY0, NZ)

    def vmem(*shape):
        return pltpu.VMEM(shape, F32)

    def sems(count):
        return pltpu.SemaphoreType.DMA((2, count))

    spec = pl.BlockSpec(memory_space=pltpu.VMEM)

    def body(*refs):
        kernel(gx_count, gy_count, *refs)

    return pl.pallas_call(
        body,
        out_shape=(
            jax.ShapeDtypeStruct(core0, F32),
            jax.ShapeDtypeStruct(core0, F32),
        ),
        in_specs=[spec] * 6,
        out_specs=(spec, spec),
        scratch_shapes=[
            vmem(2, *ext0),
            vmem(2, *ext1),
            vmem(2, *ext2),
            vmem(2, NX1 // 2, NY1, NZ),
            vmem(2, NX1 // 2, NY1, NZ),
            vmem(3, *ext0),
            vmem(*ext0),
            vmem(*ext0),
            vmem(*ext0),
            vmem(6, *ext0),
            vmem(*ext0),
            vmem(*ext0),
            vmem(*core0),
            vmem(*ext1),
            vmem(*ext1),
            vmem(*ext1),
            vmem(6, *ext1),
            vmem(*ext1),
            vmem(*ext1),
            vmem(*ext2),
            vmem(*ext2),
            vmem(*ext2),
            vmem(6, *ext2),
            vmem(*ext2),
            vmem(NY1, NZ),
            vmem(*ext0),
            vmem(TSTEPS, *ext0),
            vmem(8, NZ),
            vmem(gx_count - 1, 8, NZ),
            vmem(8, NZ),
            vmem(gy_count - 1, 8, NZ),
            vmem(TSTEPS, *ext0),
            sems(len(NEAR)),
            sems(len(WIDE)),
            sems(len(NEAR)),
            sems(len(NEAR)),
            sems(len(NEAR)),
            pltpu.SemaphoreType.DMA((2, 2, len(WIDE))),
            sems(gx_count - 1),
            sems(gy_count - 1),
            sems(len(NEAR)),
        ],
        compiler_params=pltpu.CompilerParams(collective_id=0, has_side_effects=True),
    )(log_perm, perturb, storage, base_press, well_rows, ints)


def solution(mesh):
    return jax.shard_map(
        local,
        mesh=mesh,
        in_specs=(
            P("gx", "gy", None),
            P("gx", "gy", None),
            P("gx", "gy", None),
            P(None, "gx", "gy", None),
            P(("gx", "gy"), None),
            P(("gx", "gy")),
            P(("gx", "gy")),
            P(("gx", "gy"), None),
            P(("gx", "gy")),
        ),
        out_specs=(P("gx", "gy", None), P("gx", "gy", None)),
        check_vma=False,
    )
```

```python
import jax
import jax.numpy as jnp
from jax import lax
from jax.experimental import pallas as pl
from jax.experimental.pallas import tpu as pltpu
from jax.sharding import PartitionSpec as P

TSTEPS = 2
VCYCLES = 2
SAMPLES = 512
CAP = 2
OMEGA = 0.8

F32 = jnp.float32
MESH = pl.DeviceIdType.MESH

CX0, CY0, H0, W0 = 8, 32, 5, 5
CX1, CY1, H1, HY1 = 4, 16, 10, 16
CX2, CY2, H2 = 2, 8, 5
HY = 8
NX0, NY0 = CX0 + 2 * H0, CY0 + 2 * HY
NX1, NY1 = CX1 + 2 * H1, CY1 + 2 * HY1
NX2, NY2 = CX2 + 2 * H2, CY2 + 2 * HY
NZ = 128


def ordered(offsets):
    return sorted(offsets, key=lambda o: (o[1] == 0, -abs(o[0]), o))


NEAR = ordered([(dx, dy) for dx in (-1, 0, 1) for dy in (-1, 0, 1) if (dx, dy) != (0, 0)])
WIDE = ordered([(dx, dy) for dx in range(-3, 4) for dy in (-1, 0, 1) if (dx, dy) != (0, 0)])


def span_x(dx, core, halo, width):
    if dx > 0:
        return pl.ds(halo + core - width, width), pl.ds(halo - width, width)
    if dx < 0:
        return pl.ds(halo, width), pl.ds(halo + core, width)
    return pl.ds(halo, core), pl.ds(halo, core)


def span_y(dy, core, width, halo=HY):
    if dy > 0:
        return pl.ds(halo + core - width, width), pl.ds(halo - width, width)
    if dy < 0:
        return pl.ds(halo, width), pl.ds(halo + core, width)
    return pl.ds(halo, core), pl.ds(halo, core)


def strips(ref, core_x, halo, width, core_y):
    def at(dx, dy):
        if dx != 0 and dy != 0:
            deep, rows = width - 1, 4 * -(-(width - 1) // 4)
        else:
            deep, rows = width, 4 * -(-width // 4)
        sx, tx = span_x(dx, core_x, halo, deep)
        sy, ty = span_y(dy, core_y, rows)
        if len(ref.shape) == 4:
            return ref.at[:, sx, sy], ref.at[:, tx, ty]
        return ref.at[sx, sy], ref.at[tx, ty]

    return at


def packed(ref):
    first, count = H1 // 2, CX1 // 2

    def at(dx, dy):
        if abs(dx) < 3:
            sx, tx = pl.ds(first, count), pl.ds(first - count * dx, count)
        elif dx > 0:
            sx, tx = pl.ds(first + count - 1, 1), pl.ds(0, 1)
        else:
            sx, tx = pl.ds(first, 1), pl.ds(2 * first + count - 1, 1)
        sy, ty = span_y(dy, CY1, (12, 12, 8, 4)[abs(dx)], HY1)
        if len(ref.shape) == 4:
            return ref.at[:, sx, sy], ref.at[:, tx, ty]
        return ref.at[sx, sy], ref.at[tx, ty]

    return at


def even_layers(shape):
    return (lax.broadcasted_iota(jnp.int32, shape, len(shape) - 1) & 1) == 0


def unpacked(values):
    even = even_layers(values.shape)
    return (
        jnp.where(even, values, pltpu.roll(values, 1, 1)),
        jnp.where(even, pltpu.roll(values, NZ - 1, 1), values),
    )


def swap_pair(values, stride):
    lane = lax.broadcasted_iota(jnp.int32, values.shape, values.ndim - 1)
    axis = values.ndim - 1
    return jnp.where(
        (lane & stride) == 0,
        pltpu.roll(values, NZ - stride, axis),
        pltpu.roll(values, stride, axis),
    )


def list_wells(rows_ref, ints_ref, listed):
    wells = rows_ref.shape[0]
    lane = lax.broadcasted_iota(jnp.int32, (wells, NZ), 1).astype(F32)
    well = lax.broadcasted_iota(jnp.int32, (wells, NZ), 0).astype(F32)
    across = [
        jnp.broadcast_to(ints_ref[pl.ds(k, 1), :].astype(F32), (NZ, wells)) for k in range(4)
    ]
    cell, count, owner, begin = [jnp.transpose(values) for values in across]
    fields = [cell]
    span = SAMPLES // TSTEPS
    for step in range(TSTEPS):
        total = jnp.zeros((wells, NZ), F32)
        for first in range(step * span, (step + 1) * span, NZ):
            records = rows_ref[:, pl.ds(first, NZ)]
            total = total + jnp.where(lane + float(first) < count, records, 0.0)
        total = jnp.sum(total, axis=1, keepdims=True)
        fields.append(jnp.where(begin <= float(step), total, 0.0))
    earlier = jnp.logical_and(owner == across[2], lane < well)
    rank = jnp.sum(jnp.where(earlier, 1.0, 0.0), axis=1, keepdims=True)
    listed[...] = jnp.zeros(listed.shape, F32)
    for slot in range(CAP):
        hit = jnp.logical_and(owner == lane, rank == float(slot))
        for f, field in enumerate(fields):
            listed[pl.ds(3 * slot + f, 1), :] = jnp.sum(
                jnp.where(hit, field, 0.0), axis=0, keepdims=True
            )


def place_wells(table, src_ref):
    columns = CX0 * CY0
    column = lax.broadcasted_iota(jnp.int32, (columns, NZ), 0)
    layer = lax.broadcasted_iota(jnp.int32, (NZ, NZ), 0)
    placed = [None] * TSTEPS
    for slot in range(CAP):
        cell = table[3 * slot : 3 * slot + 1].astype(jnp.int32)
        here = column == cell // NZ
        deep = jnp.where(layer == lax.rem(cell, NZ), 1.0, 0.0)
        for step in range(TSTEPS):
            weight = table[3 * slot + 1 + step : 3 * slot + 2 + step]
            part = lax.dot_general(
                jnp.where(here, weight, 0.0),
                deep,
                (((1,), (1,)), ((), ())),
                precision=lax.Precision.HIGHEST,
                preferred_element_type=F32,
            )
            placed[step] = part if placed[step] is None else placed[step] + part
    for step in range(TSTEPS):
        src_ref[step, pl.ds(H0, CX0), pl.ds(HY, CY0)] = placed[step].reshape(CX0, CY0, NZ)


def kernel(
    gx_count,
    gy_count,
    log_ref,
    pert_ref,
    stor_ref,
    press_ref,
    rows_ref,
    ints_ref,
    hess_ref,
    final_ref,
    ms0,
    ms1,
    ms2,
    pks,
    pk,
    pp,
    xa,
    xb,
    bb,
    a0,
    dinv0,
    dg0,
    r0,
    b1,
    e1a,
    e1b,
    a1,
    dinv1,
    dg1,
    b2,
    e2a,
    e2b,
    a2,
    dinv2,
    pair,
    bl,
    dps,
    listed,
    by_row,
    sorted_ref,
    by_col,
    src_ref,
    s_ms0,
    s_ms1,
    s_pp,
    s_bb,
    s_x,
    s_b1,
    s_row,
    s_col,
    s_src,
):
    gx = lax.axis_index("gx")
    gy = lax.axis_index("gy")

    def exists(dx, dy):
        tx, ty = gx + dx, gy + dy
        ok = None
        for cond in (
            [tx >= 0] * (dx < 0) + [tx < gx_count] * (dx > 0)
            + [ty >= 0] * (dy < 0) + [ty < gy_count] * (dy > 0)
        ):
            ok = cond if ok is None else jnp.logical_and(ok, cond)
        return ok

    def copies(offsets, sems, views):
        made = []
        for index, (dx, dy) in enumerate(offsets):
            source, target = views(dx, dy)
            made.append(
                (
                    dx,
                    dy,
                    pltpu.make_async_remote_copy(
                        src_ref=source,
                        dst_ref=target,
                        send_sem=sems.at[0, index],
                        recv_sem=sems.at[1, index],
                        device_id=(gx + dx, gy + dy),
                        device_id_type=MESH,
                    ),
                )
            )
        return made

    def start(made):
        for dx, dy, copy in made:
            pl.when(exists(dx, dy))(copy.start)

    def finish(made):
        for dx, dy, copy in made:
            pl.when(exists(-dx, -dy))(copy.wait_recv)
        for dx, dy, copy in made:
            pl.when(exists(dx, dy))(copy.wait_send)

    def spread(table, slots, sems, peers):
        return [
            pltpu.make_async_remote_copy(
                src_ref=table,
                dst_ref=slots.at[k],
                send_sem=sems.at[0, k],
                recv_sem=sems.at[1, k],
                device_id=peer,
                device_id_type=MESH,
            )
            for k, peer in enumerate(peers)
        ]

    def fine(ref, width):
        return strips(ref, CX0, H0, width, CY0)

    def halve(first, second, size, stride):
        pair[pl.ds(0, 2 * size), :] = first + second
        summed = pair[pl.ds(0, size, stride=2), :] + pair[pl.ds(1, size, stride=2), :]
        return 0.125 * (summed + swap_pair(summed, stride))

    def double(values, size):
        pair[pl.ds(0, size, stride=2), :] = values
        pair[pl.ds(1, size, stride=2), :] = values
        return pair[pl.ds(0, 2 * size), :]

    y0, y1 = pl.ds(HY, CY0), pl.ds(HY1, CY1)
    even = even_layers((CY1, NZ))

    for ref in (ms0, pk, pks, pp, bb):
        ref[...] = jnp.zeros(ref.shape, F32)
    for i in range(CX0):
        ms0[0, H0 + i, y0] = log_ref[i]
        ms0[1, H0 + i, y0] = stor_ref[i]
        pp[0, H0 + i, y0] = pert_ref[i]
        pp[1, H0 + i, y0] = press_ref[0, i]
        pp[2, H0 + i, y0] = press_ref[1, i]
    for f, ref in enumerate((log_ref, stor_ref)):
        means = [halve(ref[2 * i], ref[2 * i + 1], CY1, 1) for i in range(CX1)]
        for p in range(CX1 // 2):
            pks[f, H1 // 2 + p, y1] = jnp.where(even, means[2 * p], means[2 * p + 1])

    row_peers = [(lax.rem(gx + k, gx_count), gy) for k in range(1, gx_count)]
    col_peers = [(gx, lax.rem(gy + k, gy_count)) for k in range(1, gy_count)]

    barrier = pltpu.get_barrier_semaphore()
    for peer in row_peers + col_peers:
        pl.semaphore_signal(barrier, inc=1, device_id=peer, device_id_type=MESH)
    for dx, dy in WIDE:
        if dx != 0 and dy != 0:

            @pl.when(exists(dx, dy))
            def _():
                pl.semaphore_signal(
                    barrier, inc=1, device_id=(gx + dx, gy + dy), device_id_type=MESH
                )

    beside_x = jnp.minimum(gx, 3) + jnp.minimum(gx_count - 1 - gx, 3)
    beside_y = jnp.minimum(gy, 1) + jnp.minimum(gy_count - 1 - gy, 1)
    pl.semaphore_wait(barrier, beside_x * beside_y + gx_count - 1 + gy_count - 1)

    setup = [
        copies(NEAR, s_ms0, fine(ms0, W0)),
        copies(WIDE, s_ms1, packed(pks)),
        copies(NEAR, s_pp, fine(pp, 3)),
    ]
    for made in setup:
        start(made)
    for ref in (xa, src_ref, hess_ref):
        ref[...] = jnp.zeros(ref.shape, F32)
    list_wells(rows_ref, ints_ref, listed)
    row_copies = spread(listed, by_row, s_row, row_peers)
    for copy in row_copies:
        copy.start()
    def coefficients(ms, a, dinv, dg, factor, rows, core, halo, core_y, stride):
        ny = ms.shape[2]
        halo_y = (ny - core_y) // 2
        row = lax.broadcasted_iota(jnp.int32, (ny, NZ), 0) - halo_y + gy * core_y
        inside_y = jnp.logical_and(row >= 0, row < gy_count * core_y)
        lane = lax.broadcasted_iota(jnp.int32, (ny, NZ), 1)
        for i in rows:
            m = ms[0, i]
            total = ms[1, i]
            faces = []
            for other in (
                ms[0, i - 1],
                ms[0, i + 1],
                pltpu.roll(m, 1, 0),
                pltpu.roll(m, ny - 1, 0),
                pltpu.roll(m, stride, 1),
                pltpu.roll(m, NZ - stride, 1),
            ):
                faces.append(factor * jnp.exp(0.5 * (m + other)))
            faces[4] = jnp.where(lane >= stride, faces[4], 0.0)
            faces[5] = jnp.where(lane < NZ - stride, faces[5], 0.0)
            for face in faces:
                total = total + face
            place = gx * core + (i - halo)
            inside_x = jnp.logical_and(place >= 0, place < gx_count * core)
            scale = jnp.where(jnp.logical_and(inside_y, inside_x), OMEGA / total, 0.0)
            for f in range(6):
                a[f, i] = faces[f] * scale
            dinv[i] = scale
            if dg is not None:
                dg[i] = total * (1.0 / OMEGA)

    finish(setup[0])
    coefficients(ms0, a0, dinv0, dg0, 1.0, range(1, NX0 - 1), CX0, H0, CY0, 1)
    finish(setup[1])
    for f in range(2):
        for p in range(NX1 // 2):
            ms1[f, 2 * p], ms1[f, 2 * p + 1] = unpacked(pks[f, p])
        for j in range(NX2):
            ms2[f, j] = halve(ms1[f, 2 * j], ms1[f, 2 * j + 1], NY2, 2)
    coefficients(ms1, a1, dinv1, dg1, 0.25, range(1, NX1 - 1), CX1, H1, CY1, 2)
    coefficients(ms2, a2, dinv2, None, 0.0625, range(1, NX2 - 1), CX2, H2, CY2, 4)
    finish(setup[2])

    def relaxed(src, right, a, i, stride):
        ny = src.shape[0 if src.ndim == 2 else 1]
        c = src[i]
        new = (1.0 - OMEGA) * c + right
        new = new + a[0, i] * src[i - 1] + a[1, i] * src[i + 1]
        new = new + a[2, i] * pltpu.roll(c, 1, 0) + a[3, i] * pltpu.roll(c, ny - 1, 0)
        new = new + a[4, i] * pltpu.roll(c, stride, 1) + a[5, i] * pltpu.roll(c, NZ - stride, 1)
        return c, new

    def sweep(src, dst, right, a, rows, stride):
        for i in rows:
            dst[i] = relaxed(src, right(i), a, i, stride)[1]

    def around(core, halo, extra):
        return range(halo - extra, halo + core + extra)

    bb_right = lambda i: bl[i]
    b1_right = lambda i: b1[i]
    b2_right = lambda i: b2[i]

    def neighbours(ref, lead, i):
        c = ref[lead, i] if lead is not None else ref[i]
        down = ref[lead, i - 1] if lead is not None else ref[i - 1]
        up = ref[lead, i + 1] if lead is not None else ref[i + 1]
        ny = c.shape[0]
        return c, (
            down,
            up,
            pltpu.roll(c, 1, 0),
            pltpu.roll(c, ny - 1, 0),
            pltpu.roll(c, 1, 1),
            pltpu.roll(c, NZ - 1, 1),
        )

    col_copies = spread(sorted_ref, by_col, s_col, col_peers)
    src_copies = copies(NEAR, s_src, fine(src_ref, 2))

    def solve(s, carry):
        @pl.when(s < TSTEPS)
        def _():
            for i in around(CX0, H0, 2):
                change, changes = neighbours(pp, 0, i)
                press, presses = neighbours(pp, 1 + s, i)
                total = dinv0[i] * (ms0[1, i] * xa[i])
                for f in range(6):
                    total = total - a0[f, i] * (0.5 * (change + changes[f])) * (press - presses[f])
                bl[i] = total

        @pl.when(s >= TSTEPS)
        def _():
            step = 2 * TSTEPS - 1 - s
            for i in around(CX0, H0, 2):
                bl[i] = dinv0[i] * (ms0[1, i] * xa[i] + src_ref[step, i] * dps[step, i])

        for i in around(CX0, H0, 0):
            bb[i, y0] = bl[i, y0]
        xa[...] = jnp.zeros(xa.shape, F32)
        bb_copies = copies(NEAR, s_bb, fine(bb, W0 - 1))

        def cycle(c, inner):
            turn = s * VCYCLES + c
            half = lax.rem(turn, 2)
            @pl.when(c == 0)
            def _():
                for i in around(CX0, H0, 2):
                    xb[i] = bl[i]

            @pl.when(c > 0)
            def _():
                sweep(xa, xb, bb_right, a0, around(CX0, H0, 2), 1)

            sweep(xb, xa, bb_right, a0, around(CX0, H0, 1), 1)
            for i in range(CX0):
                old, new = relaxed(xa, bb_right(H0 + i), a0, H0 + i, 1)
                r0[i] = ((new - old) * dg0[H0 + i])[HY : HY + CY0]
            sides = [
                dinv1[H1 + i, y1] * halve(r0[2 * i], r0[2 * i + 1], CY1, 1) for i in range(CX1)
            ]
            for p in range(CX1 // 2):
                pk[half, H1 // 2 + p, y1] = jnp.where(even, sides[2 * p], sides[2 * p + 1])
            made = copies(WIDE, s_b1.at[half], packed(pk.at[half]))
            start(made)

            @pl.when(c == 0)
            def _():
                start(bb_copies)

            finish(made)
            for p in range(NX1 // 2):
                b1[2 * p], b1[2 * p + 1] = unpacked(pk[half, p])
            sweep(b1, e1b, b1_right, a1, around(CX1, H1, 9), 2)
            for j in range(1, NX2 - 1):
                pairs = []
                for i in (2 * j, 2 * j + 1):
                    old, new = relaxed(e1b, b1[i], a1, i, 2)
                    pairs.append((new - old) * dg1[i])
                b2[j] = dinv2[j] * halve(pairs[0], pairs[1], NY2, 2)
            sweep(b2, e2a, b2_right, a2, around(CX2, H2, 3), 4)
            sweep(e2a, e2b, b2_right, a2, around(CX2, H2, 2), 4)
            sweep(e2b, e2a, b2_right, a2, around(CX2, H2, 1), 4)
            for j in range(CX2 + 2):
                spread = double(e2a[H2 - 1 + j], NY2)
                low = H1 - 2 + 2 * j
                e1b[low] = e1b[low] + spread
                e1b[low + 1] = e1b[low + 1] + spread
            sweep(e1b, e1a, b1_right, a1, around(CX1, H1, 1), 2)
            for i in range(CX1):
                new = relaxed(e1a, b1[H1 + i], a1, H1 + i, 2)[1]
                spread = double(new[HY1 : HY1 + CY1], CY1)
                low = H0 + 2 * i
                xa[low, y0] = xa[low, y0] + spread
                xa[low + 1, y0] = xa[low + 1, y0] + spread
            made = copies(NEAR, s_x, fine(xa, W0))
            start(made)

            @pl.when(turn == 0)
            def _():
                for copy in row_copies:
                    copy.wait()
                lane = lax.broadcasted_iota(jnp.int32, (8, NZ), 1)
                total = jnp.zeros((8, NZ), F32)
                for k in range(gx_count):
                    table = listed[...] if k == 0 else by_row[k - 1]
                    owned = jnp.where(lane // gy_count == gx, table, 0.0)
                    sender = lax.rem(gx + gx_count - k, gx_count)
                    shift = lax.rem((sender - gx + gx_count) * gy_count, NZ)
                    total = total + pltpu.roll(owned, shift, 1)
                sorted_ref[...] = total
                for copy in col_copies:
                    copy.start()

            @pl.when(turn == 1)
            def _():
                for copy in col_copies:
                    copy.wait()
                lane = lax.broadcasted_iota(jnp.int32, (8, NZ), 1)
                mine = lax.rem(lane, gy_count) == gy
                total = jnp.zeros((8, NZ), F32)
                for k in range(gy_count):
                    table = sorted_ref[...] if k == 0 else by_col[k - 1]
                    sender = lax.rem(gy + gy_count - k, gy_count)
                    shift = lax.rem(sender - gy + NZ, NZ)
                    total = total + pltpu.roll(jnp.where(mine, table, 0.0), shift, 1)
                place_wells(total, src_ref)
                start(src_copies)

            @pl.when(turn == 3)
            def _():
                finish(src_copies)

            finish(made)

            @pl.when(c == 0)
            def _():
                finish(bb_copies)
                for i in around(CX0, H0, 4):
                    bl[i] = bb[i]

            sweep(xa, xb, bb_right, a0, around(CX0, H0, 4), 1)
            sweep(xb, xa, bb_right, a0, around(CX0, H0, 3), 1)
            return inner

        lax.fori_loop(0, VCYCLES, cycle, 0)

        @pl.when(s < TSTEPS)
        def _():
            for i in around(CX0, H0, 2):
                dps[s, i] = xa[i]

        @pl.when(s == TSTEPS - 1)
        def _():
            final_ref[...] = xa[pl.ds(H0, CX0), y0]
            xa[...] = jnp.zeros(xa.shape, F32)

        @pl.when(s >= TSTEPS)
        def _():
            step = 2 * TSTEPS - 1 - s
            for i in range(CX0):
                ext = H0 + i
                adjoint, adjoints = neighbours(xa, None, ext)
                press, presses = neighbours(pp, 1 + step, ext)
                total = jnp.zeros((NY0, NZ), F32)
                for f in range(6):
                    total = total + a0[f, ext] * (press - presses[f]) * (adjoint - adjoints[f])
                hess_ref[i] = hess_ref[i] - (0.5 * dg0[ext] * total)[HY : HY + CY0]

        return carry

    lax.fori_loop(0, 2 * TSTEPS, solve, 0)


def local(
    log_perm,
    perturb,
    storage,
    base_press,
    well_rows,
    well_cells,
    well_counts,
    well_owner,
    well_start,
):
    gx_count = lax.axis_size("gx")
    gy_count = lax.axis_size("gy")
    ints = jnp.stack([well_cells, well_counts, well_owner[:, 0], well_start])
    ext0 = (NX0, NY0, NZ)
    ext1 = (NX1, NY1, NZ)
    ext2 = (NX2, NY2, NZ)
    core0 = (CX0, CY0, NZ)

    def vmem(*shape):
        return pltpu.VMEM(shape, F32)

    def sems(count):
        return pltpu.SemaphoreType.DMA((2, count))

    spec = pl.BlockSpec(memory_space=pltpu.VMEM)

    def body(*refs):
        kernel(gx_count, gy_count, *refs)

    return pl.pallas_call(
        body,
        out_shape=(
            jax.ShapeDtypeStruct(core0, F32),
            jax.ShapeDtypeStruct(core0, F32),
        ),
        in_specs=[spec] * 6,
        out_specs=(spec, spec),
        scratch_shapes=[
            vmem(2, *ext0),
            vmem(2, *ext1),
            vmem(2, *ext2),
            vmem(2, NX1 // 2, NY1, NZ),
            vmem(2, NX1 // 2, NY1, NZ),
            vmem(3, *ext0),
            vmem(*ext0),
            vmem(*ext0),
            vmem(*ext0),
            vmem(6, *ext0),
            vmem(*ext0),
            vmem(*ext0),
            vmem(*core0),
            vmem(*ext1),
            vmem(*ext1),
            vmem(*ext1),
            vmem(6, *ext1),
            vmem(*ext1),
            vmem(*ext1),
            vmem(*ext2),
            vmem(*ext2),
            vmem(*ext2),
            vmem(6, *ext2),
            vmem(*ext2),
            vmem(NY1, NZ),
            vmem(*ext0),
            vmem(TSTEPS, *ext0),
            vmem(8, NZ),
            vmem(gx_count - 1, 8, NZ),
            vmem(8, NZ),
            vmem(gy_count - 1, 8, NZ),
            vmem(TSTEPS, *ext0),
            sems(len(NEAR)),
            sems(len(WIDE)),
            sems(len(NEAR)),
            sems(len(NEAR)),
            sems(len(NEAR)),
            pltpu.SemaphoreType.DMA((2, 2, len(WIDE))),
            sems(gx_count - 1),
            sems(gy_count - 1),
            sems(len(NEAR)),
        ],
        compiler_params=pltpu.CompilerParams(collective_id=0, has_side_effects=True),
    )(log_perm, perturb, storage, base_press, well_rows, ints)


def solution(mesh):
    return jax.shard_map(
        local,
        mesh=mesh,
        in_specs=(
            P("gx", "gy", None),
            P("gx", "gy", None),
            P("gx", "gy", None),
            P(None, "gx", "gy", None),
            P(("gx", "gy"), None),
            P(("gx", "gy")),
            P(("gx", "gy")),
            P(("gx", "gy"), None),
            P(("gx", "gy")),
        ),
        out_specs=(P("gx", "gy", None), P("gx", "gy", None)),
        check_vma=False,
    )
```

```python
import jax
import jax.numpy as jnp
from jax import lax
from jax.experimental import pallas as pl
from jax.experimental.pallas import tpu as pltpu
from jax.sharding import PartitionSpec as P

TSTEPS = 2
VCYCLES = 2
SAMPLES = 512
CAP = 2
OMEGA = 0.8

F32 = jnp.float32
MESH = pl.DeviceIdType.MESH

CX0, CY0, H0, W0 = 8, 32, 5, 5
CX1, CY1, H1, HY1 = 4, 16, 10, 16
CX2, CY2, H2 = 2, 8, 5
HY = 8
NX0, NY0 = CX0 + 2 * H0, CY0 + 2 * HY
NX1, NY1 = CX1 + 2 * H1, CY1 + 2 * HY1
NX2, NY2 = CX2 + 2 * H2, CY2 + 2 * HY
NZ = 128


def ordered(offsets):
    return sorted(offsets, key=lambda o: (o[1] == 0, -abs(o[0]), o))


NEAR = ordered([(dx, dy) for dx in (-1, 0, 1) for dy in (-1, 0, 1) if (dx, dy) != (0, 0)])
WIDE = ordered([(dx, dy) for dx in range(-3, 4) for dy in (-1, 0, 1) if (dx, dy) != (0, 0)])


def span_x(dx, core, halo, width):
    if dx > 0:
        return pl.ds(halo + core - width, width), pl.ds(halo - width, width)
    if dx < 0:
        return pl.ds(halo, width), pl.ds(halo + core, width)
    return pl.ds(halo, core), pl.ds(halo, core)


def span_y(dy, core, width, halo=HY):
    if dy > 0:
        return pl.ds(halo + core - width, width), pl.ds(halo - width, width)
    if dy < 0:
        return pl.ds(halo, width), pl.ds(halo + core, width)
    return pl.ds(halo, core), pl.ds(halo, core)


def strips(ref, core_x, halo, width, core_y):
    def at(dx, dy):
        if dx != 0 and dy != 0:
            deep, rows = width - 1, 4 * -(-(width - 1) // 4)
        else:
            deep, rows = width, 4 * -(-width // 4)
        sx, tx = span_x(dx, core_x, halo, deep)
        sy, ty = span_y(dy, core_y, rows)
        if len(ref.shape) == 4:
            return ref.at[:, sx, sy], ref.at[:, tx, ty]
        return ref.at[sx, sy], ref.at[tx, ty]

    return at


def packed(ref):
    first, count = H1 // 2, CX1 // 2

    def at(dx, dy):
        if abs(dx) < 3:
            sx, tx = pl.ds(first, count), pl.ds(first - count * dx, count)
        elif dx > 0:
            sx, tx = pl.ds(first + count - 1, 1), pl.ds(0, 1)
        else:
            sx, tx = pl.ds(first, 1), pl.ds(2 * first + count - 1, 1)
        sy, ty = span_y(dy, CY1, (12, 12, 8, 4)[abs(dx)], HY1)
        if len(ref.shape) == 4:
            return ref.at[:, sx, sy], ref.at[:, tx, ty]
        return ref.at[sx, sy], ref.at[tx, ty]

    return at


def even_layers(shape):
    return (lax.broadcasted_iota(jnp.int32, shape, len(shape) - 1) & 1) == 0


def unpacked(values):
    even = even_layers(values.shape)
    return (
        jnp.where(even, values, pltpu.roll(values, 1, 1)),
        jnp.where(even, pltpu.roll(values, NZ - 1, 1), values),
    )


def swap_pair(values, stride):
    lane = lax.broadcasted_iota(jnp.int32, values.shape, values.ndim - 1)
    axis = values.ndim - 1
    return jnp.where(
        (lane & stride) == 0,
        pltpu.roll(values, NZ - stride, axis),
        pltpu.roll(values, stride, axis),
    )


def list_wells(rows_ref, ints_ref, listed):
    wells = rows_ref.shape[0]
    lane = lax.broadcasted_iota(jnp.int32, (wells, NZ), 1).astype(F32)
    well = lax.broadcasted_iota(jnp.int32, (wells, NZ), 0).astype(F32)
    across = [
        jnp.broadcast_to(ints_ref[pl.ds(k, 1), :].astype(F32), (NZ, wells)) for k in range(4)
    ]
    cell, count, owner, begin = [jnp.transpose(values) for values in across]
    fields = [cell]
    span = SAMPLES // TSTEPS
    for step in range(TSTEPS):
        total = jnp.zeros((wells, NZ), F32)
        for first in range(step * span, (step + 1) * span, NZ):
            records = rows_ref[:, pl.ds(first, NZ)]
            total = total + jnp.where(lane + float(first) < count, records, 0.0)
        total = jnp.sum(total, axis=1, keepdims=True)
        fields.append(jnp.where(begin <= float(step), total, 0.0))
    earlier = jnp.logical_and(owner == across[2], lane < well)
    rank = jnp.sum(jnp.where(earlier, 1.0, 0.0), axis=1, keepdims=True)
    listed[...] = jnp.zeros(listed.shape, F32)
    for slot in range(CAP):
        hit = jnp.logical_and(owner == lane, rank == float(slot))
        for f, field in enumerate(fields):
            listed[pl.ds(3 * slot + f, 1), :] = jnp.sum(
                jnp.where(hit, field, 0.0), axis=0, keepdims=True
            )


def place_wells(table, src_ref):
    columns = CX0 * CY0
    column = lax.broadcasted_iota(jnp.int32, (columns, NZ), 0)
    layer = lax.broadcasted_iota(jnp.int32, (NZ, NZ), 0)
    placed = [None] * TSTEPS
    for slot in range(CAP):
        cell = table[3 * slot : 3 * slot + 1].astype(jnp.int32)
        here = column == cell // NZ
        deep = jnp.where(layer == lax.rem(cell, NZ), 1.0, 0.0)
        for step in range(TSTEPS):
            weight = table[3 * slot + 1 + step : 3 * slot + 2 + step]
            part = lax.dot_general(
                jnp.where(here, weight, 0.0),
                deep,
                (((1,), (1,)), ((), ())),
                precision=lax.Precision.HIGHEST,
                preferred_element_type=F32,
            )
            placed[step] = part if placed[step] is None else placed[step] + part
    for step in range(TSTEPS):
        src_ref[step, pl.ds(H0, CX0), pl.ds(HY, CY0)] = placed[step].reshape(CX0, CY0, NZ)


def kernel(
    gx_count,
    gy_count,
    log_ref,
    pert_ref,
    stor_ref,
    press_ref,
    rows_ref,
    ints_ref,
    hess_ref,
    final_ref,
    ms0,
    ms1,
    ms2,
    pks,
    pk,
    pp,
    xa,
    xb,
    bb,
    a0,
    dinv0,
    dg0,
    r0,
    b1,
    e1a,
    e1b,
    a1,
    dinv1,
    dg1,
    b2,
    e2a,
    e2b,
    a2,
    dinv2,
    pair,
    bl,
    dps,
    listed,
    by_row,
    sorted_ref,
    by_col,
    src_ref,
    s_ms0,
    s_ms1,
    s_pp,
    s_bb,
    s_x,
    s_b1,
    s_row,
    s_col,
    s_src,
):
    gx = lax.axis_index("gx")
    gy = lax.axis_index("gy")

    def exists(dx, dy):
        tx, ty = gx + dx, gy + dy
        ok = None
        for cond in (
            [tx >= 0] * (dx < 0) + [tx < gx_count] * (dx > 0)
            + [ty >= 0] * (dy < 0) + [ty < gy_count] * (dy > 0)
        ):
            ok = cond if ok is None else jnp.logical_and(ok, cond)
        return ok

    def copies(offsets, sems, views):
        made = []
        for index, (dx, dy) in enumerate(offsets):
            source, target = views(dx, dy)
            made.append(
                (
                    dx,
                    dy,
                    pltpu.make_async_remote_copy(
                        src_ref=source,
                        dst_ref=target,
                        send_sem=sems.at[0, index],
                        recv_sem=sems.at[1, index],
                        device_id=(gx + dx, gy + dy),
                        device_id_type=MESH,
                    ),
                )
            )
        return made

    def start(made):
        for dx, dy, copy in made:
            pl.when(exists(dx, dy))(copy.start)

    def finish(made):
        for dx, dy, copy in made:
            pl.when(exists(-dx, -dy))(copy.wait_recv)
        for dx, dy, copy in made:
            pl.when(exists(dx, dy))(copy.wait_send)

    def spread(table, slots, sems, peers):
        return [
            pltpu.make_async_remote_copy(
                src_ref=table,
                dst_ref=slots.at[k],
                send_sem=sems.at[0, k],
                recv_sem=sems.at[1, k],
                device_id=peer,
                device_id_type=MESH,
            )
            for k, peer in enumerate(peers)
        ]

    def fine(ref, width):
        return strips(ref, CX0, H0, width, CY0)

    def halve(first, second, size, stride):
        pair[pl.ds(0, 2 * size), :] = first + second
        summed = pair[pl.ds(0, size, stride=2), :] + pair[pl.ds(1, size, stride=2), :]
        return 0.125 * (summed + swap_pair(summed, stride))

    def double(values, size):
        pair[pl.ds(0, size, stride=2), :] = values
        pair[pl.ds(1, size, stride=2), :] = values
        return pair[pl.ds(0, 2 * size), :]

    y0, y1 = pl.ds(HY, CY0), pl.ds(HY1, CY1)
    even = even_layers((CY1, NZ))

    for ref in (ms0, pk, pks, pp, bb):
        ref[...] = jnp.zeros(ref.shape, F32)
    for i in range(CX0):
        ms0[0, H0 + i, y0] = log_ref[i]
        ms0[1, H0 + i, y0] = stor_ref[i]
        pp[0, H0 + i, y0] = pert_ref[i]
        pp[1, H0 + i, y0] = press_ref[0, i]
        pp[2, H0 + i, y0] = press_ref[1, i]
    for f, ref in enumerate((log_ref, stor_ref)):
        means = [halve(ref[2 * i], ref[2 * i + 1], CY1, 1) for i in range(CX1)]
        for p in range(CX1 // 2):
            pks[f, H1 // 2 + p, y1] = jnp.where(even, means[2 * p], means[2 * p + 1])

    row_peers = [(lax.rem(gx + k, gx_count), gy) for k in range(1, gx_count)]
    col_peers = [(gx, lax.rem(gy + k, gy_count)) for k in range(1, gy_count)]

    barrier = pltpu.get_barrier_semaphore()
    for peer in row_peers + col_peers:
        pl.semaphore_signal(barrier, inc=1, device_id=peer, device_id_type=MESH)
    for dx, dy in WIDE:
        if dx != 0 and dy != 0:

            @pl.when(exists(dx, dy))
            def _():
                pl.semaphore_signal(
                    barrier, inc=1, device_id=(gx + dx, gy + dy), device_id_type=MESH
                )

    beside_x = jnp.minimum(gx, 3) + jnp.minimum(gx_count - 1 - gx, 3)
    beside_y = jnp.minimum(gy, 1) + jnp.minimum(gy_count - 1 - gy, 1)
    pl.semaphore_wait(barrier, beside_x * beside_y + gx_count - 1 + gy_count - 1)

    setup = [
        copies(NEAR, s_ms0, fine(ms0, W0)),
        copies(WIDE, s_ms1, packed(pks)),
        copies(NEAR, s_pp, fine(pp, 3)),
    ]
    for made in setup:
        start(made)
    for ref in (xa, src_ref, hess_ref):
        ref[...] = jnp.zeros(ref.shape, F32)
    list_wells(rows_ref, ints_ref, listed)
    row_copies = spread(listed, by_row, s_row, row_peers)
    for copy in row_copies:
        copy.start()
    def coefficients(ms, a, dinv, dg, factor, rows, core, halo, core_y, stride):
        ny = ms.shape[2]
        halo_y = (ny - core_y) // 2
        row = lax.broadcasted_iota(jnp.int32, (ny, NZ), 0) - halo_y + gy * core_y
        inside_y = jnp.logical_and(row >= 0, row < gy_count * core_y)
        lane = lax.broadcasted_iota(jnp.int32, (ny, NZ), 1)
        for i in rows:
            m = ms[0, i]
            total = ms[1, i]
            faces = []
            for other in (
                ms[0, i - 1],
                ms[0, i + 1],
                pltpu.roll(m, 1, 0),
                pltpu.roll(m, ny - 1, 0),
                pltpu.roll(m, stride, 1),
                pltpu.roll(m, NZ - stride, 1),
            ):
                faces.append(factor * jnp.exp(0.5 * (m + other)))
            faces[4] = jnp.where(lane >= stride, faces[4], 0.0)
            faces[5] = jnp.where(lane < NZ - stride, faces[5], 0.0)
            for face in faces:
                total = total + face
            place = gx * core + (i - halo)
            inside_x = jnp.logical_and(place >= 0, place < gx_count * core)
            scale = jnp.where(jnp.logical_and(inside_y, inside_x), OMEGA / total, 0.0)
            for f in range(6):
                a[f, i] = faces[f] * scale
            dinv[i] = scale
            if dg is not None:
                dg[i] = total * (1.0 / OMEGA)

    finish(setup[0])
    coefficients(ms0, a0, dinv0, dg0, 1.0, range(1, NX0 - 1), CX0, H0, CY0, 1)
    finish(setup[1])
    for f in range(2):
        for p in range(NX1 // 2):
            ms1[f, 2 * p], ms1[f, 2 * p + 1] = unpacked(pks[f, p])
        for j in range(NX2):
            ms2[f, j] = halve(ms1[f, 2 * j], ms1[f, 2 * j + 1], NY2, 2)
    coefficients(ms1, a1, dinv1, dg1, 0.25, range(1, NX1 - 1), CX1, H1, CY1, 2)
    coefficients(ms2, a2, dinv2, None, 0.0625, range(1, NX2 - 1), CX2, H2, CY2, 4)
    finish(setup[2])

    def relaxed(src, right, a, i, stride):
        ny = src.shape[0 if src.ndim == 2 else 1]
        c = src[i]
        new = (1.0 - OMEGA) * c + right
        new = new + a[0, i] * src[i - 1] + a[1, i] * src[i + 1]
        new = new + a[2, i] * pltpu.roll(c, 1, 0) + a[3, i] * pltpu.roll(c, ny - 1, 0)
        new = new + a[4, i] * pltpu.roll(c, stride, 1) + a[5, i] * pltpu.roll(c, NZ - stride, 1)
        return c, new

    def sweep(src, dst, right, a, rows, stride):
        for i in rows:
            dst[i] = relaxed(src, right(i), a, i, stride)[1]

    def around(core, halo, extra):
        return range(halo - extra, halo + core + extra)

    bb_right = lambda i: bl[i]
    b1_right = lambda i: b1[i]
    b2_right = lambda i: b2[i]

    def neighbours(ref, lead, i):
        c = ref[lead, i] if lead is not None else ref[i]
        down = ref[lead, i - 1] if lead is not None else ref[i - 1]
        up = ref[lead, i + 1] if lead is not None else ref[i + 1]
        ny = c.shape[0]
        return c, (
            down,
            up,
            pltpu.roll(c, 1, 0),
            pltpu.roll(c, ny - 1, 0),
            pltpu.roll(c, 1, 1),
            pltpu.roll(c, NZ - 1, 1),
        )

    col_copies = spread(sorted_ref, by_col, s_col, col_peers)
    src_copies = copies(NEAR, s_src, fine(src_ref, 2))

    def solve(s, carry):
        @pl.when(s < TSTEPS)
        def _():
            for i in around(CX0, H0, 2):
                change, changes = neighbours(pp, 0, i)
                press, presses = neighbours(pp, 1 + s, i)
                total = dinv0[i] * (ms0[1, i] * xa[i])
                for f in range(6):
                    total = total - a0[f, i] * (0.5 * (change + changes[f])) * (press - presses[f])
                bl[i] = total

        @pl.when(s >= TSTEPS)
        def _():
            step = 2 * TSTEPS - 1 - s
            for i in around(CX0, H0, 2):
                bl[i] = dinv0[i] * (ms0[1, i] * xa[i] + src_ref[step, i] * dps[step, i])

        for i in around(CX0, H0, 0):
            bb[i, y0] = bl[i, y0]
        xa[...] = jnp.zeros(xa.shape, F32)
        bb_copies = copies(NEAR, s_bb, fine(bb, W0 - 1))

        def cycle(c, inner):
            turn = s * VCYCLES + c
            half = lax.rem(turn, 2)
            @pl.when(c == 0)
            def _():
                for i in around(CX0, H0, 2):
                    xb[i] = bl[i]

            @pl.when(c > 0)
            def _():
                sweep(xa, xb, bb_right, a0, around(CX0, H0, 2), 1)

            sweep(xb, xa, bb_right, a0, around(CX0, H0, 1), 1)
            for i in range(CX0):
                old, new = relaxed(xa, bb_right(H0 + i), a0, H0 + i, 1)
                r0[i] = ((new - old) * dg0[H0 + i])[HY : HY + CY0]
            sides = [
                dinv1[H1 + i, y1] * halve(r0[2 * i], r0[2 * i + 1], CY1, 1) for i in range(CX1)
            ]
            for p in range(CX1 // 2):
                pk[half, H1 // 2 + p, y1] = jnp.where(even, sides[2 * p], sides[2 * p + 1])
            made = copies(WIDE, s_b1.at[half], packed(pk.at[half]))
            start(made)
            finish(made)

            @pl.when(c == 0)
            def _():
                start(bb_copies)

            for p in range(NX1 // 2):
                b1[2 * p], b1[2 * p + 1] = unpacked(pk[half, p])
            sweep(b1, e1b, b1_right, a1, around(CX1, H1, 9), 2)
            for j in range(1, NX2 - 1):
                pairs = []
                for i in (2 * j, 2 * j + 1):
                    old, new = relaxed(e1b, b1[i], a1, i, 2)
                    pairs.append((new - old) * dg1[i])
                b2[j] = dinv2[j] * halve(pairs[0], pairs[1], NY2, 2)
            sweep(b2, e2a, b2_right, a2, around(CX2, H2, 3), 4)
            sweep(e2a, e2b, b2_right, a2, around(CX2, H2, 2), 4)
            sweep(e2b, e2a, b2_right, a2, around(CX2, H2, 1), 4)
            for j in range(CX2 + 2):
                spread = double(e2a[H2 - 1 + j], NY2)
                low = H1 - 2 + 2 * j
                e1b[low] = e1b[low] + spread
                e1b[low + 1] = e1b[low + 1] + spread
            sweep(e1b, e1a, b1_right, a1, around(CX1, H1, 1), 2)
            for i in range(CX1):
                new = relaxed(e1a, b1[H1 + i], a1, H1 + i, 2)[1]
                spread = double(new[HY1 : HY1 + CY1], CY1)
                low = H0 + 2 * i
                xa[low, y0] = xa[low, y0] + spread
                xa[low + 1, y0] = xa[low + 1, y0] + spread
            made = copies(NEAR, s_x, fine(xa, W0))
            start(made)

            @pl.when(turn == 0)
            def _():
                for copy in row_copies:
                    copy.wait()
                lane = lax.broadcasted_iota(jnp.int32, (8, NZ), 1)
                total = jnp.zeros((8, NZ), F32)
                for k in range(gx_count):
                    table = listed[...] if k == 0 else by_row[k - 1]
                    owned = jnp.where(lane // gy_count == gx, table, 0.0)
                    sender = lax.rem(gx + gx_count - k, gx_count)
                    shift = lax.rem((sender - gx + gx_count) * gy_count, NZ)
                    total = total + pltpu.roll(owned, shift, 1)
                sorted_ref[...] = total
                for copy in col_copies:
                    copy.start()

            @pl.when(turn == 1)
            def _():
                for copy in col_copies:
                    copy.wait()
                lane = lax.broadcasted_iota(jnp.int32, (8, NZ), 1)
                mine = lax.rem(lane, gy_count) == gy
                total = jnp.zeros((8, NZ), F32)
                for k in range(gy_count):
                    table = sorted_ref[...] if k == 0 else by_col[k - 1]
                    sender = lax.rem(gy + gy_count - k, gy_count)
                    shift = lax.rem(sender - gy + NZ, NZ)
                    total = total + pltpu.roll(jnp.where(mine, table, 0.0), shift, 1)
                place_wells(total, src_ref)
                start(src_copies)

            @pl.when(turn == 3)
            def _():
                finish(src_copies)

            finish(made)

            @pl.when(c == 0)
            def _():
                finish(bb_copies)
                for i in around(CX0, H0, 4):
                    bl[i] = bb[i]

            sweep(xa, xb, bb_right, a0, around(CX0, H0, 4), 1)
            sweep(xb, xa, bb_right, a0, around(CX0, H0, 3), 1)
            return inner

        lax.fori_loop(0, VCYCLES, cycle, 0)

        @pl.when(s < TSTEPS)
        def _():
            for i in around(CX0, H0, 2):
                dps[s, i] = xa[i]

        @pl.when(s == TSTEPS - 1)
        def _():
            final_ref[...] = xa[pl.ds(H0, CX0), y0]
            xa[...] = jnp.zeros(xa.shape, F32)

        @pl.when(s >= TSTEPS)
        def _():
            step = 2 * TSTEPS - 1 - s
            for i in range(CX0):
                ext = H0 + i
                adjoint, adjoints = neighbours(xa, None, ext)
                press, presses = neighbours(pp, 1 + step, ext)
                total = jnp.zeros((NY0, NZ), F32)
                for f in range(6):
                    total = total + a0[f, ext] * (press - presses[f]) * (adjoint - adjoints[f])
                hess_ref[i] = hess_ref[i] - (0.5 * dg0[ext] * total)[HY : HY + CY0]

        return carry

    lax.fori_loop(0, 2 * TSTEPS, solve, 0)


def local(
    log_perm,
    perturb,
    storage,
    base_press,
    well_rows,
    well_cells,
    well_counts,
    well_owner,
    well_start,
):
    gx_count = lax.axis_size("gx")
    gy_count = lax.axis_size("gy")
    ints = jnp.stack([well_cells, well_counts, well_owner[:, 0], well_start])
    ext0 = (NX0, NY0, NZ)
    ext1 = (NX1, NY1, NZ)
    ext2 = (NX2, NY2, NZ)
    core0 = (CX0, CY0, NZ)

    def vmem(*shape):
        return pltpu.VMEM(shape, F32)

    def sems(count):
        return pltpu.SemaphoreType.DMA((2, count))

    spec = pl.BlockSpec(memory_space=pltpu.VMEM)

    def body(*refs):
        kernel(gx_count, gy_count, *refs)

    return pl.pallas_call(
        body,
        out_shape=(
            jax.ShapeDtypeStruct(core0, F32),
            jax.ShapeDtypeStruct(core0, F32),
        ),
        in_specs=[spec] * 6,
        out_specs=(spec, spec),
        scratch_shapes=[
            vmem(2, *ext0),
            vmem(2, *ext1),
            vmem(2, *ext2),
            vmem(2, NX1 // 2, NY1, NZ),
            vmem(2, NX1 // 2, NY1, NZ),
            vmem(3, *ext0),
            vmem(*ext0),
            vmem(*ext0),
            vmem(*ext0),
            vmem(6, *ext0),
            vmem(*ext0),
            vmem(*ext0),
            vmem(*core0),
            vmem(*ext1),
            vmem(*ext1),
            vmem(*ext1),
            vmem(6, *ext1),
            vmem(*ext1),
            vmem(*ext1),
            vmem(*ext2),
            vmem(*ext2),
            vmem(*ext2),
            vmem(6, *ext2),
            vmem(*ext2),
            vmem(NY1, NZ),
            vmem(*ext0),
            vmem(TSTEPS, *ext0),
            vmem(8, NZ),
            vmem(gx_count - 1, 8, NZ),
            vmem(8, NZ),
            vmem(gy_count - 1, 8, NZ),
            vmem(TSTEPS, *ext0),
            sems(len(NEAR)),
            sems(len(WIDE)),
            sems(len(NEAR)),
            sems(len(NEAR)),
            sems(len(NEAR)),
            pltpu.SemaphoreType.DMA((2, 2, len(WIDE))),
            sems(gx_count - 1),
            sems(gy_count - 1),
            sems(len(NEAR)),
        ],
        compiler_params=pltpu.CompilerParams(collective_id=0, has_side_effects=True),
    )(log_perm, perturb, storage, base_press, well_rows, ints)


def solution(mesh):
    return jax.shard_map(
        local,
        mesh=mesh,
        in_specs=(
            P("gx", "gy", None),
            P("gx", "gy", None),
            P("gx", "gy", None),
            P(None, "gx", "gy", None),
            P(("gx", "gy"), None),
            P(("gx", "gy")),
            P(("gx", "gy")),
            P(("gx", "gy"), None),
            P(("gx", "gy")),
        ),
        out_specs=(P("gx", "gy", None), P("gx", "gy", None)),
        check_vma=False,
    )
```
